256 devices in a mesh: shot: 4 (over x), dom: 64 (over z, y, core).
Axes of the slice: x: 4, y: 4, z: 8, core: 2. Of those that a mesh axis runs over, the one named last changes fastest.
Arguments:
- forward: float32 [8, 9, 125, 16384], P('shot', None, None, 'dom'), may hold values from -6 to 6
- adjoint: float32 [8, 9, 125, 16384], P('shot', None, None, 'dom'), may hold values from -6 to 6
- material: float32 [3, 125, 16384], P(None, None, 'dom'), may hold values from 0.5 to 2
- counts: int32 [64], P('dom'), may hold values from 64 to 256, as said below
- send_list: int32 [64, 4, 32], P('dom'), may hold values from 0 to 256, as said below
- neighbours: int32 [64, 1536], P('dom'), may hold values from 0 to 1665, as said below
Outputs:
- forward_next: float32 [8, 9, 125, 16384], P('shot', None, None, 'dom')
- adjoint_next: float32 [8, 9, 125, 16384], P('shot', None, None, 'dom')
- gradient: float32 [3, 125, 16384], P(None, None, 'dom')
The draws below stay inside these ranges and needn't reach their ends.
Inputs may be any that keep to these rules, and one draw needn't show every extreme that they name: Device d holds counts[d] octants in its first slots, in Morton order of its tree; some device holds 256 and some device holds only one layer, 64. `send_list`: entry [d, s, p] is the slot of device d's octant on lateral side s (-x, +x, -y, +y) at position p = (horizontal coordinate along the side) * 4 + layer, or 256 where the position holds no octant; every listed slot is live. `neighbours`: codes as in the reference program: a code below 1536 names a live local face; a ghost code names a position whose octant the neighbouring tree lists; 1665 marks an absorbing boundary and is also given for every face of a slot that is not live.
All inputs are finite; a program needn't handle non-finite values.
Results may differ from the reference program's by a relative error of at most 0.0003.
Values sent between devices are 32-bit elements; how exact they have to be, the bound alone decides.
A program may use at most 192 MiB of HBM per device.

```python
import math
import jax
import jax.numpy as jnp
import numpy as np
from jax import lax

BOX = 8
EZ = 4
DEV_Y = 4
NODES = 125
FIELDS = 9
OCT_DEV = 256
SHOTS = 8
OCTANTS = 16384
N_DOM = 64


def forest_layout(key):
    layers = EZ
    devices = N_DOM
    slot_count = BOX * BOX * layers
    side_length = BOX * layers
    rows_of_trees = devices // DEV_Y
    layout_key = jax.random.fold_in(key, 4242)
    key_level, key_vary, key_full, key_low = jax.random.split(layout_key, 4)
    device_ids = jnp.arange(devices, dtype=jnp.int32)
    tall_tree = jax.random.randint(key_level, (devices,), 0, 5) == 0
    full_device = jax.random.randint(key_full, (), 0, devices)
    low_device = (full_device + 1 + jax.random.randint(key_low, (), 0, devices - 1)) % devices
    levels = jnp.where(tall_tree, layers, 1)
    variation = jax.random.randint(key_vary, (devices, BOX, BOX), -1, 2)
    heights = jnp.clip(levels[:, None, None] + variation, 1, layers)
    heights = jnp.where((device_ids == full_device)[:, None, None], layers, heights)
    heights = jnp.where((device_ids == low_device)[:, None, None], 1, heights)
    grid_x, grid_y, grid_z = jnp.meshgrid(jnp.arange(BOX, dtype=jnp.int32), jnp.arange(BOX, dtype=jnp.int32), jnp.arange(layers, dtype=jnp.int32), indexing='ij')
    morton = jnp.zeros_like(grid_x)
    for bit_number in range(5):
        morton = morton + ((grid_x >> bit_number & 1) << 3 * bit_number + 2)
        morton = morton + ((grid_y >> bit_number & 1) << 3 * bit_number + 1)
        morton = morton + ((grid_z >> bit_number & 1) << 3 * bit_number)
    live_cells = grid_z[None] < heights[:, :, :, None]
    sort_key = morton[None] + jnp.where(live_cells, 0, 65536)
    position_of = jnp.argsort(sort_key.reshape(devices, slot_count), axis=1).astype(jnp.int32)
    slot_of = jnp.argsort(position_of, axis=1).astype(jnp.int32)
    slot_cells = slot_of.reshape(devices, BOX, BOX, layers)
    counts = jnp.sum(live_cells.reshape(devices, slot_count).astype(jnp.int32), axis=1).astype(jnp.int32)
    free_code = 6 * slot_count + 4 * side_length
    absorb_code = free_code + 1
    tree_x = device_ids // DEV_Y
    tree_y = device_ids % DEV_Y
    grids = (grid_x, grid_y, grid_z)
    extents = (BOX, BOX, layers)
    per_face = []
    for face_id in range(6):
        direction = face_id // 2
        sign = 1 if face_id % 2 == 1 else -1
        opposite = face_id + 1 if face_id % 2 == 0 else face_id - 1
        moved_coord = grids[direction] + sign
        inside = (moved_coord >= 0) & (moved_coord < extents[direction])
        next_live = jnp.roll(live_cells, -sign, axis=1 + direction)
        next_slot = jnp.roll(slot_cells, -sign, axis=1 + direction)
        local_value = jnp.where(next_live, opposite * slot_count + next_slot, free_code)
        edge = 0 if sign > 0 else BOX - 1
        if direction == 2:
            outside_value = jnp.full(live_cells.shape, absorb_code if sign < 0 else free_code, jnp.int32)
        elif direction == 0:
            exists = (tree_x + sign >= 0) & (tree_x + sign < rows_of_trees)
            column = jnp.roll(heights, -sign * DEV_Y, axis=0)[:, edge, :]
            ghost_live = grid_z[None] < column[:, None, :, None]
            ghost_value = 6 * slot_count + face_id * side_length + grid_y * layers + grid_z
            outside_value = jnp.where(exists[:, None, None, None], jnp.where(ghost_live, ghost_value[None], free_code), absorb_code)
        else:
            exists = (tree_y + sign >= 0) & (tree_y + sign < DEV_Y)
            column = jnp.roll(heights, -sign, axis=0)[:, :, edge]
            ghost_live = grid_z[None] < column[:, :, None, None]
            ghost_value = 6 * slot_count + face_id * side_length + grid_x * layers + grid_z
            outside_value = jnp.where(exists[:, None, None, None], jnp.where(ghost_live, ghost_value[None], free_code), absorb_code)
        combined = jnp.where(inside[None], local_value, outside_value)
        combined = jnp.where(live_cells, combined, absorb_code)
        per_face.append(combined.reshape(devices, slot_count))
    stacked = jnp.stack(per_face, axis=1)
    gather_index = jnp.broadcast_to(position_of[:, None, :], stacked.shape)
    neighbours = jnp.take_along_axis(stacked, gather_index, axis=2).reshape(devices, 6 * slot_count).astype(jnp.int32)
    side_slots = (slot_cells[:, 0], slot_cells[:, BOX - 1], slot_cells[:, :, 0], slot_cells[:, :, BOX - 1])
    side_lives = (live_cells[:, 0], live_cells[:, BOX - 1], live_cells[:, :, 0], live_cells[:, :, BOX - 1])
    send_list = jnp.stack([jnp.where(alive, slots_here, slot_count).reshape(devices, side_length) for alive, slots_here in zip(side_lives, side_slots)], axis=1).astype(jnp.int32)
    return (counts, send_list, neighbours)


def draw_counts(key, part):
    return forest_layout(key)[0]


def draw_send_list(key, part):
    return forest_layout(key)[1]


def draw_neighbours(key, part):
    return forest_layout(key)[2]


def block_scale(stream_key, shape, cuts, low, top_value):
    factor_of = 1.0
    for dim, shards_of in cuts:
        steps = jax.random.uniform(jax.random.fold_in(jax.random.fold_in(stream_key, 6), dim), (shards_of,), jnp.float32, low / len(cuts), top_value / len(cuts))
        factor_of = factor_of * jnp.repeat(jnp.exp(steps), shape[dim] // shards_of).reshape((-1,) + (1,) * (len(shape) - 1 - dim))
    return factor_of


def centred(own_key, extent, scale, bound, cuts=(), kind=jnp.bfloat16):
    drawn = scale * jax.random.normal(own_key, extent, jnp.float32)
    if cuts:
        drawn = drawn * block_scale(own_key, extent, cuts, -0.22, 0.18)
    return jnp.clip(drawn, -bound, bound).astype(kind)


def setup_inputs(seed: int = 0) -> dict:
    key_list = jax.random.split(jax.random.key(seed), 7)
    forward = centred(key_list[0], (SHOTS, FIELDS, NODES, OCTANTS), 1.0, 6.0, ((0, 4), (3, 64)), jnp.float32)
    adjoint = centred(key_list[1], (SHOTS, FIELDS, NODES, OCTANTS), 1.0, 6.0, ((0, 4), (3, 64)), jnp.float32)
    material = jnp.clip(jnp.exp(math.log(2.0) - 1.3862944 * jax.random.uniform(key_list[2], (3, NODES, OCTANTS), jnp.float32) ** block_scale(key_list[2], (3, NODES, OCTANTS), ((2, 64),), -0.2, 0.2)), 0.5, 2.0)
    counts = draw_counts(jax.random.fold_in(key_list[6], 71), 0)
    send_list = draw_send_list(jax.random.fold_in(key_list[6], 71), 0)
    neighbours = draw_neighbours(jax.random.fold_in(key_list[6], 71), 0)
    return {"forward": forward, "adjoint": adjoint, "material": material, "counts": counts, "send_list": send_list, "neighbours": neighbours}


step_size = 0.01
lift_weight = 10.0
highest = lax.Precision.HIGHEST
stress_slots = ((3, 8, 7), (8, 4, 6), (7, 6, 5))
symmetric_pairs = ((0, 0), (1, 1), (2, 2), (1, 2), (0, 2), (0, 1))

def derivative_matrix():
    points = np.array([-1.0, -np.sqrt(3.0 / 7.0), 0.0, np.sqrt(3.0 / 7.0), 1.0])
    barycentric = np.array([1.0 / np.prod([points[a] - points[b] for b in range(5) if b != a]) for a in range(5)])
    matrix = np.zeros((5, 5))
    for a in range(5):
        for b in range(5):
            if a != b:
                matrix[a, b] = barycentric[b] / barycentric[a] / (points[a] - points[b])
        matrix[a, a] = -np.sum(matrix[a])
    return jnp.asarray(matrix, dtype=jnp.float32)

def split_nodes(values):
    return values.reshape(values.shape[:2] + (5, 5, 5) + values.shape[3:])

def derivative_parts(states):
    matrix = derivative_matrix()
    shaped = split_nodes(states)
    along_x = jnp.einsum('ai,sfijk...->sfajk...', matrix, shaped, precision=highest)
    along_y = jnp.einsum('aj,sfijk...->sfiak...', matrix, shaped, precision=highest)
    along_z = jnp.einsum('ak,sfijk...->sfija...', matrix, shaped, precision=highest)
    return tuple((part.reshape(states.shape) for part in (along_x, along_y, along_z)))

def volume_terms(derivs, medium):
    lame_first = medium[:, 0]
    shear_modulus = medium[:, 1]
    buoyancy = medium[:, 2]
    divergence = derivs[0][:, 0] + derivs[1][:, 1] + derivs[2][:, 2]
    stress_div = [sum((derivs[d][:, stress_slots[a][d]] for d in range(3))) for a in range(3)]
    rates = [derivs[a][:, b] + derivs[b][:, a] for a, b in symmetric_pairs]
    flux_rows = [buoyancy * part for part in stress_div]
    for pair_id, (a, b) in enumerate(symmetric_pairs):
        stress_row = shear_modulus * rates[pair_id]
        if a == b:
            stress_row = stress_row + lame_first * divergence
        flux_rows.append(stress_row)
    return (jnp.stack(flux_rows, axis=1), (divergence, rates, stress_div))

def material_partials(rate_parts, dual):
    divergence, rates, stress_div = rate_parts
    pressure_part = divergence * (dual[:, 3] + dual[:, 4] + dual[:, 5])
    shear_part = sum((rates[n] * dual[:, 3 + n] for n in range(6)))
    buoyancy_part = sum((stress_div[a] * dual[:, a] for a in range(3)))
    return jnp.stack([pressure_part, shear_part, buoyancy_part], axis=1)

def face_of(values, face_id):
    shaped = split_nodes(values)
    position = 0 if face_id % 2 == 0 else 4
    picked = lax.index_in_dim(shaped, position, axis=2 + face_id // 2, keepdims=False)
    return picked.reshape(values.shape[:2] + (25,) + values.shape[3:])

def face_traces(values):
    return jnp.concatenate([face_of(values, face_id) for face_id in range(6)], axis=-1)

def add_face(tendency, face_id, values):
    shaped = values.reshape(values.shape[:2] + (5, 5) + values.shape[3:])
    selector = [slice(None)] * tendency.ndim
    selector[2 + face_id // 2] = 0 if face_id % 2 == 0 else 4
    return tendency.at[tuple(selector)].add(shaped)

def surface_terms(volume, jump_all, medium_faces, slot_count):
    tendency = split_nodes(volume)
    for face_id in range(6):
        direction = face_id // 2
        normal = -1.0 if face_id % 2 == 0 else 1.0
        window = slice(face_id * slot_count, (face_id + 1) * slot_count)
        jump_piece = jump_all[..., window]
        lame_first = medium_faces[:, 0, :, window]
        shear_modulus = medium_faces[:, 1, :, window]
        buoyancy = medium_faces[:, 2, :, window]
        wave_speed = jnp.sqrt((lame_first + 2.0 * shear_modulus) * buoyancy)
        flux_rows = [buoyancy * jump_piece[:, stress_slots[a][direction]] for a in range(3)]
        for a, b in symmetric_pairs:
            flux_terms = []
            if a == b:
                flux_terms.append(lame_first * jump_piece[:, direction])
            if direction == a:
                flux_terms.append(shear_modulus * jump_piece[:, b])
            if direction == b:
                flux_terms.append(shear_modulus * jump_piece[:, a])
            flux_rows.append(sum(flux_terms) if flux_terms else None)
        corrections = []
        for field_id in range(9):
            amount = wave_speed * jump_piece[:, field_id]
            if flux_rows[field_id] is not None:
                amount = amount + normal * flux_rows[field_id]
            corrections.append(0.5 * lift_weight * amount)
        tendency = add_face(tendency, face_id, jnp.stack(corrections, axis=1))
    return tendency.reshape(volume.shape)

def shift_devices(values, offset):
    padding = jnp.zeros((abs(offset),) + values.shape[1:], values.dtype)
    if offset > 0:
        return jnp.concatenate([padding, values[:-offset]], axis=0)
    return jnp.concatenate([values[-offset:], padding], axis=0)

def ghost_reference(traces, send_list, slot_count):
    sent = []
    for side_id in range(4):
        listed = send_list[:, side_id]
        target = jnp.where(listed < slot_count, side_id * slot_count + listed, 6 * slot_count)
        target = jnp.broadcast_to(target[:, None, None, :], traces.shape[:3] + (listed.shape[1],))
        sent.append(jnp.take_along_axis(traces, target, axis=3, mode='fill', fill_value=0.0))
    pieces = [shift_devices(sent[side_id], offset) for offset, side_id in ((DEV_Y, 1), (-DEV_Y, 0), (1, 3), (-1, 2))]
    return jnp.concatenate(pieces, axis=3)

def tendency_reference(states, medium, medium_faces, send_list, neighbours):
    slot_count = states.shape[3]
    derivs = derivative_parts(states)
    volume, rate_parts = volume_terms(derivs, medium)
    traces = face_traces(states)
    sources = jnp.concatenate([traces, ghost_reference(traces, send_list, slot_count)], axis=3)
    free_code = sources.shape[3]
    target = jnp.broadcast_to(neighbours[:, None, None, :], traces.shape)
    exterior = jnp.take_along_axis(sources, target, axis=3, mode='fill', fill_value=0.0)
    free_mask = (neighbours == free_code).astype(jnp.float32)[:, None, None, :]
    jump_all = exterior - traces
    jump_all = jnp.concatenate([jump_all[:, :3] * (1.0 - free_mask), jump_all[:, 3:] * (1.0 + free_mask)], axis=1)
    return (surface_terms(volume, jump_all, medium_faces, slot_count), rate_parts)

def reference(forward, adjoint, material, counts, send_list, neighbours):
    slot_count = OCT_DEV
    devices = N_DOM
    live_mask = (jnp.arange(slot_count, dtype=jnp.int32)[None, :] < counts[:, None]).astype(jnp.float32)
    medium = jnp.transpose(material.reshape(3, 125, devices, slot_count), (2, 0, 1, 3))
    medium_faces = face_traces(medium)

    def per_device(values):
        shaped = jnp.transpose(values.reshape(9, 125, devices, slot_count), (2, 0, 1, 3))
        return shaped * live_mask[:, None, None, :]

    def restore(values):
        return jnp.transpose(values, (1, 2, 0, 3)).reshape(values.shape[1], 125, devices * slot_count)

    def advance(states):
        return tendency_reference(states, medium, medium_faces, send_list, neighbours)

    def one_shot(pair):
        states = per_device(pair[0])
        duals = per_device(pair[1])
        forward_rate, forward_parts = advance(states)
        adjoint_rate, unused_parts = advance(duals)
        forward_mid = states + step_size * forward_rate
        adjoint_mid = duals + step_size * adjoint_rate
        forward_rate2, forward_parts2 = advance(forward_mid)
        adjoint_rate2, unused_parts2 = advance(adjoint_mid)
        forward_end = 0.5 * states + 0.5 * (forward_mid + step_size * forward_rate2)
        adjoint_end = 0.5 * duals + 0.5 * (adjoint_mid + step_size * adjoint_rate2)
        partial_value = material_partials(forward_parts, duals) + material_partials(forward_parts2, adjoint_mid)
        return (restore(forward_end), restore(adjoint_end), partial_value)
    forward_next, adjoint_next, partials = lax.map(one_shot, (forward, adjoint))
    gradient = 0.5 * step_size * lax.optimization_barrier(jnp.sum(partials, axis=0))
    gradient = jnp.transpose(gradient, (1, 2, 0, 3)).reshape(3, 125, devices * slot_count)
    return (forward_next, adjoint_next, gradient)
```

```python
import functools

import jax
import jax.numpy as jnp
import numpy as np
from jax import lax
from jax.experimental import pallas as pl
from jax.experimental.pallas import tpu as pltpu
from jax.sharding import PartitionSpec as P

MESH = pl.DeviceIdType.MESH
PAIRS = ((0, 0), (1, 1), (2, 2), (1, 2), (0, 2), (0, 1))
SLOTS = ((3, 8, 7), (8, 4, 6), (7, 6, 5))
N_DOM = 64
N_SHOT = 4
BLOCKS = 30
SIDE_ROWS = 8 * BLOCKS
QUARTER = 96
ROUTES = ((4, 1), (-4, 0), (1, 3), (-1, 2))
F32 = jnp.float32


def derivative_matrix():
    points = np.array([-1.0, -np.sqrt(3.0 / 7.0), 0.0, np.sqrt(3.0 / 7.0), 1.0])
    weights = [1.0 / np.prod([points[a] - points[b] for b in range(5) if b != a]) for a in range(5)]
    matrix = np.zeros((5, 5))
    for a in range(5):
        for b in range(5):
            if a != b:
                matrix[a, b] = weights[b] / weights[a] / (points[a] - points[b])
        matrix[a, a] = -np.sum(matrix[a])
    return matrix


D = derivative_matrix()


def line_derivative(u):
    e0, o0 = u[0] + u[4], u[0] - u[4]
    e1, o1 = u[1] + u[3], u[1] - u[3]
    even = [
        float((D[a, 0] + D[a, 4]) / 2) * e0 + float((D[a, 1] + D[a, 3]) / 2) * e1 + float(D[a, 2]) * u[2]
        for a in (0, 1)
    ]
    odd = [float((D[a, 0] - D[a, 4]) / 2) * o0 + float((D[a, 1] - D[a, 3]) / 2) * o1 for a in (0, 1, 2)]
    return [odd[0] + even[0], odd[1] + even[1], odd[2], odd[1] - even[1], odd[0] - even[0]]


def rows(field, node, count=1, nodes=125):
    start = 8 * (nodes * field + node)
    if not isinstance(start, int):
        start = pl.multiple_of(start, 8)
    return pl.ds(start, 8 * count)


def face_node(face, p, q):
    fixed = 0 if face % 2 == 0 else 4
    if face < 2:
        return 25 * fixed + 5 * p + q
    if face < 4:
        return 25 * p + 5 * fixed + q
    return 25 * p + 5 * q + fixed


def iotas():
    row = lax.broadcasted_iota(jnp.int32, (8, 128), 0)
    lane = lax.broadcasted_iota(jnp.int32, (8, 128), 1)
    return row, lane, row // 4


def pick(x, index):
    return jnp.take_along_axis(x, index, axis=1, mode="promise_in_bounds")


def other_half(x):
    return pltpu.roll(x, 4, 0)


def pack_sides(u, lists, s):
    row, lane, half = iotas()
    group = half * 4 + lane // 32
    for side in range(4):
        listed = jnp.broadcast_to(lists[0, side : side + 1, :], (8, 128))
        index = listed & 127
        from_half = listed >> 7
        same = from_half == half
        crossed = from_half == 1 - half

        def body(p, carry, side=side, index=index, same=same, crossed=crossed):
            packed = None
            for column in range(45):
                q, field = divmod(column, 9)
                x = u[rows(field, face_node(side, p, q)), :]
                value = jnp.where(same, pick(x, index), jnp.where(crossed, pick(other_half(x), index), 0.0))
                t = column % 8
                packed = value if t == 0 else jnp.where(group == t, value, packed)
                if t == 7 or column == 44:
                    s[rows(side * BLOCKS + p * 6 + column // 8, 0, nodes=1), :] = packed
            return carry

        lax.fori_loop(0, 5, body, 0)


def pack_kernel(count, fw, ad, mat, lists, u, m, s):
    row, lane, half = iotas()
    live = [lane + 128 * h < count[0] for h in range(2)]

    def per_block(block, carry, size=8):
        for kind, src in enumerate((fw, ad)):
            for shot in range(2):
                for h in range(2):
                    x = src[pl.ds(32 * block + 2 * h + shot, size, stride=4), :]
                    u[pl.ds(64 * block + 4 * h + 2 * kind + shot, size, stride=8), :] = jnp.where(live[h][:size], x, 0.0)
        return carry

    lax.fori_loop(0, 140, per_block, 0)
    per_block(140, 0, 5)

    def per_kind(c, carry):
        for h in range(2):
            for block in range(16):
                size = 8 if block < 15 else 5
                x = 0.01 * mat[c, pl.ds(8 * block, size), pl.ds(128 * h, 128)]
                for ks in range(4):
                    m[pl.ds(c * 1000 + 64 * block + 4 * h + ks, size, stride=8), :] = x
        return carry

    lax.fori_loop(0, 3, per_kind, 0)
    pack_sides(u, lists, s)


X_FIELDS = (0, 1, 2, 3, 8, 7)
Y_FIELDS = (0, 1, 2, 8, 4, 6)
Z_FIELDS = (0, 1, 2, 7, 6, 5)


def volume(u, m, a, gx, gy, gz, part):
    def x_lines(j, carry):
        for slot, field in enumerate(X_FIELDS):
            lines = [u[rows(field, 25 * i + 5 * j, 5), :] for i in range(5)]
            for i, value in enumerate(line_derivative(lines)):
                gx[rows(slot, 25 * i + 5 * j, 5), :] = value
        return carry

    lax.fori_loop(0, 5, x_lines, 0)

    def slab(i, carry):
        for slot, field in enumerate(Y_FIELDS):
            lines = [u[rows(field, 25 * i + 5 * j, 5), :] for j in range(5)]
            for j, value in enumerate(line_derivative(lines)):
                gy[rows(slot, 5 * j, 5, nodes=25), :] = value
        for slot, field in enumerate(Z_FIELDS):
            for j in range(5):
                lines = [u[rows(field, 25 * i + 5 * j + k), :] for k in range(5)]
                for k, value in enumerate(line_derivative(lines)):
                    gz[rows(slot, 5 * j + k, nodes=25), :] = value

        def line(j, inner):
            for k in range(5):
                n = 25 * i + 5 * j + k
                x = [gx[rows(slot, n), :] for slot in range(6)]
                y = [gy[rows(slot, 5 * j + k, nodes=25), :] for slot in range(6)]
                z = [gz[rows(slot, 5 * j + k, nodes=25), :] for slot in range(6)]
                state = [u[rows(field, n), :] for field in range(9)]
                lam, mu, buoy = (m[rows(c, n), :] for c in range(3))
                divergence = x[0] + y[1] + z[2]
                sdiv = [x[3] + y[3] + z[3], x[4] + y[4] + z[4], x[5] + y[5] + z[5]]
                shear = [y[2] + z[1], x[2] + z[0], x[1] + y[0]]
                diagonal = [x[0], y[1], z[2]]
                pressure = lam * divergence
                twice = mu + mu
                for b in range(3):
                    a[rows(b, n), :] = state[b] + buoy * sdiv[b]
                    a[rows(3 + b, n), :] = state[3 + b] + (pressure + twice * diagonal[b])
                    a[rows(6 + b, n), :] = state[6 + b] + mu * shear[b]
                dual = [pltpu.roll(v, 6, 0) for v in state]
                part[rows(0, n), :] = divergence * (dual[3] + dual[4] + dual[5])
                normal = diagonal[0] * dual[3] + diagonal[1] * dual[4] + diagonal[2] * dual[5]
                tangent = shear[0] * dual[6] + shear[1] * dual[7] + shear[2] * dual[8]
                part[rows(1, n), :] = (normal + normal) + tangent
                part[rows(2, n), :] = sdiv[0] * dual[0] + sdiv[1] * dual[1] + sdiv[2] * dual[2]
            return inner

        lax.fori_loop(0, 5, line, 0)
        return carry

    lax.fori_loop(0, 5, slab, 0)


def sum_shots(part, total, earlier=None):
    for c in range(3):
        for block in range(16):
            size = 8 if block < 15 else 5
            for h in range(2):
                start = 1000 * c + 64 * block + 4 * h
                value = part[pl.ds(start, size, stride=8), :] + part[pl.ds(start + 1, size, stride=8), :]
                where = (pl.ds(128 * c + 8 * block, size), pl.ds(128 * h, 128))
                if earlier is not None:
                    value = value + earlier[where]
                if size < 8:
                    total[pl.ds(128 * c + 8 * block, 8), pl.ds(128 * h, 128)] = jnp.zeros((8, 128), F32)
                total[where] = value


def dom_peer(offset):
    d = lax.axis_index("dom")
    return lax.rem(d + offset + N_DOM, N_DOM)


def greet(shots):
    barrier = pltpu.get_barrier_semaphore()
    for offset, side in ROUTES:
        pl.semaphore_signal(barrier, inc=1, device_id={"dom": dom_peer(offset)}, device_id_type=MESH)
    if shots:
        me = lax.axis_index("shot")
        for step in range(1, N_SHOT):
            peer = lax.rem(me + step, N_SHOT)
            pl.semaphore_signal(barrier, inc=1, device_id={"shot": peer}, device_id_type=MESH)
    pl.semaphore_wait(barrier, 4 + (3 if shots else 0))


def start_sides(s, ghosts, send_sem, recv_sem):
    copies = []
    for b, (offset, side) in enumerate(ROUTES):
        copy = pltpu.make_async_remote_copy(
            src_ref=s.at[pl.ds(side * SIDE_ROWS, SIDE_ROWS)],
            dst_ref=ghosts.at[pl.ds(b * SIDE_ROWS, SIDE_ROWS)],
            send_sem=send_sem.at[b],
            recv_sem=recv_sem.at[b],
            device_id={"dom": dom_peer(offset)},
            device_id_type=MESH,
        )
        copy.start()
        copies.append(copy)
    return copies


def first_kernel(s, u, m, a, ghosts, total, gx, gy, gz, part, send_sem, recv_sem):
    greet(False)
    copies = start_sides(s, ghosts, send_sem, recv_sem)
    volume(u, m, a, gx, gy, gz, part)
    sum_shots(part, total)
    for copy in copies:
        copy.wait()


def second_kernel(
    s, u, m, earlier, a, ghosts, gradient, gx, gy, gz, part, mine, theirs, send_sem, recv_sem, grad_send, grad_recv
):
    greet(True)
    copies = start_sides(s, ghosts, send_sem, recv_sem)
    volume(u, m, a, gx, gy, gz, part)
    sum_shots(part, mine, earlier)
    me = lax.axis_index("shot")
    own = pl.ds(pl.multiple_of(me * QUARTER, 8), QUARTER)
    outgoing = []
    for step in range(1, N_SHOT):
        peer = lax.rem(me + step, N_SHOT)
        copy = pltpu.make_async_remote_copy(
            src_ref=mine.at[pl.ds(pl.multiple_of(peer * QUARTER, 8), QUARTER)],
            dst_ref=theirs.at[step - 1],
            send_sem=grad_send.at[step - 1],
            recv_sem=grad_recv.at[step - 1],
            device_id={"shot": peer},
            device_id_type=MESH,
        )
        copy.start()
        outgoing.append(copy)
    for copy in outgoing:
        copy.wait_recv()
    summed = mine[own, :] + theirs[0] + theirs[1] + theirs[2]
    gradient[own, :] = 0.005 * summed
    spread = []
    for step in range(1, N_SHOT):
        peer = lax.rem(me + step, N_SHOT)
        copy = pltpu.make_async_remote_copy(
            src_ref=gradient.at[own],
            dst_ref=gradient.at[own],
            send_sem=grad_send.at[2 + step],
            recv_sem=grad_recv.at[2 + step],
            device_id={"shot": peer},
            device_id_type=MESH,
        )
        copy.start()
        spread.append(copy)
    for copy in outgoing:
        copy.wait_send()
    for copy in spread:
        copy.wait()
    for copy in copies:
        copy.wait()


def correct_face(face, p, u, m, source, target, mirror, ext):
    axis = face // 2
    sign = -1.0 if face % 2 == 0 else 1.0
    velocity_scale, stress_scale = mirror
    for q in range(5):
        n = face_node(face, p, q)
        lam, mu, buoy = (m[rows(c, n), :] for c in range(3))
        speed = 5.0 * jnp.sqrt((lam + 2.0 * mu) * buoy)
        speed_v = speed * velocity_scale
        speed_s = speed * stress_scale
        kb = (5.0 * sign) * buoy * stress_scale
        signed = (5.0 * sign) * velocity_scale
        kl = lam * signed
        km = mu * signed
        jump = [ext(q, field) - u[rows(field, n), :] for field in range(9)]
        for b in range(3):
            place = rows(b, n)
            target[place, :] = source[place, :] + (kb * jump[SLOTS[b][axis]] + speed_v * jump[b])
        pressure = kl * jump[axis]
        for pair, (b, c) in enumerate(PAIRS):
            amount = speed_s * jump[3 + pair]
            if b == c:
                amount = amount + pressure
            if axis == b and axis == c:
                amount = amount + (km + km) * jump[axis]
            elif axis == b:
                amount = amount + km * jump[c]
            elif axis == c:
                amount = amount + km * jump[b]
            place = rows(3 + pair, n)
            target[place, :] = source[place, :] + amount


def surface(u, m, ghosts, codes, a, target, scratch):
    row, lane, half = iotas()
    d = lax.axis_index("dom")
    here = [(d - offset >= 0) & (d - offset < N_DOM) for offset, side in ROUTES]
    present = [jnp.where(h, 1, 0) for h in here]

    def copy_slab(i, carry):
        for field in range(9):
            place = rows(field, 25 * i, 25)
            target[place, :] = a[place, :]
        return carry

    lax.fori_loop(1, 4, copy_slab, 0)

    face_codes, odd = [], jnp.zeros((8, 128), F32)
    for face in range(6):
        low = jnp.broadcast_to(codes[0:1, 256 * face : 256 * face + 128], (8, 128))
        high = jnp.broadcast_to(codes[0:1, 256 * face + 128 : 256 * face + 256], (8, 128))
        code = jnp.where(half == 0, low, high)
        face_codes.append(code)
        usual = ((code >> 8) == (face ^ 1)) | (code >= 1664)
        if face < 4:
            usual = usual | ((code >> 5) == 48 + face)
        odd = odd + jnp.where(usual, 0.0, 1.0)
    general = jnp.sum(odd) > 0.0

    def scales(code):
        free = code == 1664
        return jnp.where(free, 0.0, 1.0), jnp.where(free, 2.0, 1.0)

    @pl.when(jnp.logical_not(general))
    def _():
        for face in range(6):
            code = face_codes[face]
            opposite = face ^ 1
            local = (code >> 8) == opposite
            index = code & 127
            same = ((code >> 7) & 1) == half
            ghost = ghost_index = None
            if face < 4:
                ghost = ((code >> 5) == 48 + face) & (jnp.broadcast_to(present[face], (8, 128)) == 1)
                ghost_index = [(code & 31) + 32 * c for c in range(4)]
            mirror = scales(code)

            def body(p, carry, face=face, opposite=opposite, local=local, index=index, same=same, ghost=ghost,
                     ghost_index=ghost_index, mirror=mirror):
                cache = {}

                def ext(q, field):
                    x = u[rows(field, face_node(opposite, p, q)), :]
                    value = jnp.where(same, pick(x, index), pick(other_half(x), index))
                    outside = 0.0
                    if ghost is not None:
                        block, t = divmod(9 * q + field, 8)
                        if (block, t // 4) not in cache:
                            if block not in cache:
                                g = ghosts[rows(face * BLOCKS + 6 * p + block, 0, nodes=1), :]
                                cache[block] = (g, other_half(g))
                            g, swapped = cache[block]
                            cache[block, t // 4] = jnp.where(half == t // 4, g, swapped)
                        outside = jnp.where(ghost, pick(cache[block, t // 4], ghost_index[t % 4]), 0.0)
                    return jnp.where(local, value, outside)

                correct_face(face, p, u, m, a if face < 2 else target, target, mirror, ext)
                return carry

            lax.fori_loop(0, 5, body, 0)

    @pl.when(general)
    def _():
        for face in range(6):
            code = face_codes[face]
            index = code & 127
            from_half = (code >> 7) & 1
            mirror = scales(code)

            def body(p, carry, face=face, code=code, index=index, from_half=from_half, mirror=mirror):
                def column_body(column, inner):
                    q = column // 9
                    field = column - 9 * q
                    value = jnp.zeros((8, 128), F32)
                    for g in range(6):
                        x = u[rows(field, face_node(g, p, q)), :]
                        found = jnp.where(from_half == half, pick(x, index), pick(other_half(x), index))
                        value = jnp.where((code >> 8) == g, found, value)
                    block = column // 8
                    t = column - 8 * block
                    upper = t // 4
                    for b in range(4):
                        x = ghosts[rows(b * BLOCKS + 6 * p + block, 0, nodes=1), :]
                        x = jnp.where(half == upper, x, other_half(x))
                        found = pick(x, (code & 31) + 32 * (t - 4 * upper))
                        mask = ((code >> 5) == 48 + b) & (jnp.broadcast_to(present[b], (8, 128)) == 1)
                        value = jnp.where(mask, found, value)
                    scratch[rows(column, 0, nodes=1), :] = value
                    return inner

                lax.fori_loop(0, 45, column_body, 0)

                def ext(q, field):
                    return scratch[rows(9 * q + field, 0, nodes=1), :]

                correct_face(face, p, u, m, a if face < 2 else target, target, mirror, ext)
                return carry

            lax.fori_loop(0, 5, body, 0)


def middle_kernel(u, m, ghosts, codes, a, lists, target, s, scratch):
    surface(u, m, ghosts, codes, a, target, scratch)
    pack_sides(target, lists, s)


def last_kernel(u, m, ghosts, codes, a, start, reduced, fw, ad, gradient, end, scratch):
    surface(u, m, ghosts, codes, a, end, scratch)

    def per_block(block, carry, size=8):
        for kind, out in enumerate((fw, ad)):
            for shot in range(2):
                for h in range(2):
                    place = pl.ds(64 * block + 4 * h + 2 * kind + shot, size, stride=8)
                    value = 0.5 * start[place, :] + 0.5 * end[place, :]
                    out[pl.ds(32 * block + 2 * h + shot, size, stride=4), :] = value
        return carry

    lax.fori_loop(0, 140, per_block, 0)
    per_block(140, 0, 5)
    for c in range(3):
        gradient[c, :, :] = reduced[pl.ds(128 * c, 125), :]


def vmem(count):
    return [pl.BlockSpec(memory_space=pltpu.VMEM)] * count


def shape(*dims):
    return jax.ShapeDtypeStruct(dims, F32)


STATE = shape(9000, 128)
SIDES = shape(4 * SIDE_ROWS, 128)
VOLUME_SCRATCH = [
    pltpu.VMEM((6000, 128), F32),
    pltpu.VMEM((1200, 128), F32),
    pltpu.VMEM((1200, 128), F32),
    pltpu.VMEM((3000, 128), F32),
]
ANY = pl.BlockSpec(memory_space=pl.ANY)


def pack_call(counts, forward, adjoint, material, lists):
    return pl.pallas_call(
        pack_kernel,
        out_shape=(STATE, shape(3000, 128), SIDES),
        in_specs=[pl.BlockSpec(memory_space=pltpu.SMEM)] + vmem(4),
        out_specs=tuple(vmem(3)),
        name="pack",
    )(counts, forward, adjoint, material, lists)


def first_call(sides, u, m):
    return pl.pallas_call(
        first_kernel,
        out_shape=(STATE, SIDES, shape(384, 256)),
        in_specs=[ANY] + vmem(2),
        out_specs=(vmem(1)[0], ANY, vmem(1)[0]),
        scratch_shapes=VOLUME_SCRATCH + [pltpu.SemaphoreType.DMA((4,)), pltpu.SemaphoreType.DMA((4,))],
        compiler_params=pltpu.CompilerParams(collective_id=0, has_side_effects=True),
        name="first",
    )(sides, u, m)


def second_call(sides, u, m, earlier):
    return pl.pallas_call(
        second_kernel,
        out_shape=(STATE, SIDES, shape(384, 256)),
        in_specs=[ANY] + vmem(3),
        out_specs=(vmem(1)[0], ANY, vmem(1)[0]),
        scratch_shapes=VOLUME_SCRATCH
        + [
            pltpu.VMEM((384, 256), F32),
            pltpu.VMEM((3, QUARTER, 256), F32),
            pltpu.SemaphoreType.DMA((4,)),
            pltpu.SemaphoreType.DMA((4,)),
            pltpu.SemaphoreType.DMA((6,)),
            pltpu.SemaphoreType.DMA((6,)),
        ],
        compiler_params=pltpu.CompilerParams(collective_id=1, has_side_effects=True),
        name="second",
    )(sides, u, m, earlier)


def middle_call(u, m, ghosts, codes, a, lists):
    return pl.pallas_call(
        middle_kernel,
        out_shape=(STATE, SIDES),
        in_specs=vmem(6),
        out_specs=tuple(vmem(2)),
        scratch_shapes=[pltpu.VMEM((360, 128), F32)],
        name="middle",
    )(u, m, ghosts, codes, a, lists)


def last_call(u, m, ghosts, codes, a, start, reduced):
    return pl.pallas_call(
        last_kernel,
        out_shape=(shape(4500, 128), shape(4500, 128), shape(3, 125, 256)),
        in_specs=vmem(7),
        out_specs=tuple(vmem(3)),
        scratch_shapes=[pltpu.VMEM((9000, 128), F32), pltpu.VMEM((360, 128), F32)],
        name="last",
    )(u, m, ghosts, codes, a, start, reduced)


def as_rows(x):
    return x.reshape(2, 9, 125, 2, 128).transpose(1, 2, 3, 0, 4).reshape(4500, 128)


def as_array(x):
    return x.reshape(9, 125, 2, 2, 128).transpose(3, 0, 1, 2, 4).reshape(2, 9, 125, 256)


def shards(forward, adjoint, material, counts, send_list, neighbours):
    lists = jnp.tile(send_list, (1, 1, 4))
    u0, m, sides = pack_call(counts, as_rows(forward), as_rows(adjoint), material, lists)
    a1, ghosts, earlier = first_call(sides, u0, m)
    u1, sides2 = middle_call(u0, m, ghosts, neighbours, a1, lists)
    a2, ghosts2, reduced = second_call(sides2, u1, m, earlier)
    fw, ad, gradient = last_call(u1, m, ghosts2, neighbours, a2, u0, reduced)
    return as_array(fw), as_array(ad), gradient


def solution(mesh):
    placed = (
        P("shot", None, None, "dom"),
        P("shot", None, None, "dom"),
        P(None, None, "dom"),
        P("dom"),
        P("dom", None, None),
        P("dom", None),
    )
    return jax.shard_map(
        shards,
        mesh=mesh,
        in_specs=placed,
        out_specs=placed[:3],
        check_vma=False,
    )
```

```python
import functools

import jax
import jax.numpy as jnp
import numpy as np
from jax import lax
from jax.experimental import pallas as pl
from jax.experimental.pallas import tpu as pltpu
from jax.sharding import PartitionSpec as P

MESH = pl.DeviceIdType.MESH
PAIRS = ((0, 0), (1, 1), (2, 2), (1, 2), (0, 2), (0, 1))
SLOTS = ((3, 8, 7), (8, 4, 6), (7, 6, 5))
N_DOM = 64
N_SHOT = 4
BLOCKS = 30
SIDE_ROWS = 8 * BLOCKS
QUARTER = 96
ROUTES = ((4, 1), (-4, 0), (1, 3), (-1, 2))
F32 = jnp.float32


def derivative_matrix():
    points = np.array([-1.0, -np.sqrt(3.0 / 7.0), 0.0, np.sqrt(3.0 / 7.0), 1.0])
    weights = [1.0 / np.prod([points[a] - points[b] for b in range(5) if b != a]) for a in range(5)]
    matrix = np.zeros((5, 5))
    for a in range(5):
        for b in range(5):
            if a != b:
                matrix[a, b] = weights[b] / weights[a] / (points[a] - points[b])
        matrix[a, a] = -np.sum(matrix[a])
    return matrix


D = derivative_matrix()


def line_derivative(u):
    e0, o0 = u[0] + u[4], u[0] - u[4]
    e1, o1 = u[1] + u[3], u[1] - u[3]
    even = [
        float((D[a, 0] + D[a, 4]) / 2) * e0 + float((D[a, 1] + D[a, 3]) / 2) * e1 + float(D[a, 2]) * u[2]
        for a in (0, 1)
    ]
    odd = [float((D[a, 0] - D[a, 4]) / 2) * o0 + float((D[a, 1] - D[a, 3]) / 2) * o1 for a in (0, 1, 2)]
    return [odd[0] + even[0], odd[1] + even[1], odd[2], odd[1] - even[1], odd[0] - even[0]]


def rows(field, node, count=1, nodes=125):
    start = 8 * (nodes * field + node)
    if not isinstance(start, int):
        start = pl.multiple_of(start, 8)
    return pl.ds(start, 8 * count)


def face_node(face, p, q):
    fixed = 0 if face % 2 == 0 else 4
    if face < 2:
        return 25 * fixed + 5 * p + q
    if face < 4:
        return 25 * p + 5 * fixed + q
    return 25 * p + 5 * q + fixed


def iotas():
    row = lax.broadcasted_iota(jnp.int32, (8, 128), 0)
    lane = lax.broadcasted_iota(jnp.int32, (8, 128), 1)
    return row, lane, row // 4


def pick(x, index):
    return jnp.take_along_axis(x, index, axis=1, mode="promise_in_bounds")


def other_half(x):
    return pltpu.roll(x, 4, 0)


def pack_sides(u, lists, s):
    row, lane, half = iotas()
    group = half * 4 + lane // 32
    for side in range(4):
        listed = jnp.tile(jnp.broadcast_to(lists[0, side : side + 1, :], (8, 32)), (1, 4))
        index = listed & 127
        from_half = listed >> 7
        here = from_half == half
        listed_slot = listed < 256

        def body(p, carry, side=side, index=index, here=here, listed_slot=listed_slot):
            packed = None
            for column in range(45):
                q, field = divmod(column, 9)
                x = u[rows(field, face_node(side, p, q)), :]
                value = pick(x, index)
                value = jnp.where(here, value, other_half(value))
                t = column % 8
                packed = value if t == 0 else jnp.where(group == t, value, packed)
                if t == 7 or column == 44:
                    s[rows(side * BLOCKS + p * 6 + column // 8, 0, nodes=1), :] = jnp.where(listed_slot, packed, 0.0)
            return carry

        lax.fori_loop(0, 5, body, 0)


def state_copies(packed, arrays, sems, inward):
    view = packed.reshape(1125, 8, 128)
    copies = []
    for kind, array in enumerate(arrays):
        for h in range(2):
            inside, outside = view.at[:, pl.ds(4 * h + 2 * kind, 2), :], array.at[:, h]
            pair = (outside, inside) if inward else (inside, outside)
            copies.append(pltpu.make_async_copy(*pair, sems.at[2 * kind + h]))
    return copies


def pack_kernel(count, fw, ad, mat, lists, u, m, s, sems):
    row, lane, half = iotas()
    copies = state_copies(u, (fw, ad), sems, True)
    for copy in copies:
        copy.start()

    def per_kind(c, carry):
        for h in range(2):
            for block in range(16):
                size = 8 if block < 15 else 5
                x = 0.01 * mat[c, pl.ds(8 * block, size), pl.ds(128 * h, 128)]
                for ks in range(4):
                    m[pl.ds(c * 1000 + 64 * block + 4 * h + ks, size, stride=8), :] = x
        return carry

    lax.fori_loop(0, 3, per_kind, 0)
    for copy in copies:
        copy.wait()
    live = lane + 128 * half < count[0]

    def mask(group, carry):
        for n in range(25):
            place = rows(0, 25 * group + n)
            u[place, :] = jnp.where(live, u[place, :], 0.0)
        return carry

    lax.fori_loop(0, 45, mask, 0)
    pack_sides(u, lists, s)


X_FIELDS = (0, 1, 2, 3, 8, 7)
Y_FIELDS = (0, 1, 2, 8, 4, 6)
Z_FIELDS = (0, 1, 2, 7, 6, 5)


def volume(u, m, a, gx, gy, gz, part):
    def x_lines(j, carry):
        for slot, field in enumerate(X_FIELDS):
            lines = [u[rows(field, 25 * i + 5 * j, 5), :] for i in range(5)]
            for i, value in enumerate(line_derivative(lines)):
                gx[rows(slot, 25 * i + 5 * j, 5), :] = value
        return carry

    lax.fori_loop(0, 5, x_lines, 0)

    def slab(i, carry):
        for slot, field in enumerate(Y_FIELDS):
            lines = [u[rows(field, 25 * i + 5 * j, 5), :] for j in range(5)]
            for j, value in enumerate(line_derivative(lines)):
                gy[rows(slot, 5 * j, 5, nodes=25), :] = value
        for slot, field in enumerate(Z_FIELDS):
            for j in range(5):
                lines = [u[rows(field, 25 * i + 5 * j + k), :] for k in range(5)]
                for k, value in enumerate(line_derivative(lines)):
                    gz[rows(slot, 5 * j + k, nodes=25), :] = value

        def line(j, inner):
            for k in range(5):
                n = 25 * i + 5 * j + k
                x = [gx[rows(slot, n), :] for slot in range(6)]
                y = [gy[rows(slot, 5 * j + k, nodes=25), :] for slot in range(6)]
                z = [gz[rows(slot, 5 * j + k, nodes=25), :] for slot in range(6)]
                state = [u[rows(field, n), :] for field in range(9)]
                lam, mu, buoy = (m[rows(c, n), :] for c in range(3))
                divergence = x[0] + y[1] + z[2]
                sdiv = [x[3] + y[3] + z[3], x[4] + y[4] + z[4], x[5] + y[5] + z[5]]
                shear = [y[2] + z[1], x[2] + z[0], x[1] + y[0]]
                diagonal = [x[0], y[1], z[2]]
                pressure = lam * divergence
                twice = mu + mu
                for b in range(3):
                    a[rows(b, n), :] = state[b] + buoy * sdiv[b]
                    a[rows(3 + b, n), :] = state[3 + b] + (pressure + twice * diagonal[b])
                    a[rows(6 + b, n), :] = state[6 + b] + mu * shear[b]
                dual = [pltpu.roll(v, 6, 0) for v in state]
                part[rows(0, n), :] = divergence * (dual[3] + dual[4] + dual[5])
                normal = diagonal[0] * dual[3] + diagonal[1] * dual[4] + diagonal[2] * dual[5]
                tangent = shear[0] * dual[6] + shear[1] * dual[7] + shear[2] * dual[8]
                part[rows(1, n), :] = (normal + normal) + tangent
                part[rows(2, n), :] = sdiv[0] * dual[0] + sdiv[1] * dual[1] + sdiv[2] * dual[2]
            return inner

        lax.fori_loop(0, 5, line, 0)
        return carry

    lax.fori_loop(0, 5, slab, 0)


def sum_shots(part, total, earlier=None):
    for c in range(3):
        for block in range(16):
            size = 8 if block < 15 else 5
            for h in range(2):
                start = 1000 * c + 64 * block + 4 * h
                value = part[pl.ds(start, size, stride=8), :] + part[pl.ds(start + 1, size, stride=8), :]
                where = (pl.ds(128 * c + 8 * block, size), pl.ds(128 * h, 128))
                if earlier is not None:
                    value = value + earlier[where]
                if size < 8:
                    total[pl.ds(128 * c + 8 * block, 8), pl.ds(128 * h, 128)] = jnp.zeros((8, 128), F32)
                total[where] = value


def dom_peer(offset):
    d = lax.axis_index("dom")
    return lax.rem(d + offset + N_DOM, N_DOM)


def greet(shots):
    barrier = pltpu.get_barrier_semaphore()
    for offset, side in ROUTES:
        pl.semaphore_signal(barrier, inc=1, device_id={"dom": dom_peer(offset)}, device_id_type=MESH)
    if shots:
        me = lax.axis_index("shot")
        for step in range(1, N_SHOT):
            peer = lax.rem(me + step, N_SHOT)
            pl.semaphore_signal(barrier, inc=1, device_id={"shot": peer}, device_id_type=MESH)
    pl.semaphore_wait(barrier, 4 + (3 if shots else 0))


def start_sides(s, ghosts, send_sem, recv_sem):
    copies = []
    for b, (offset, side) in enumerate(ROUTES):
        copy = pltpu.make_async_remote_copy(
            src_ref=s.at[pl.ds(side * SIDE_ROWS, SIDE_ROWS)],
            dst_ref=ghosts.at[pl.ds(b * SIDE_ROWS, SIDE_ROWS)],
            send_sem=send_sem.at[b],
            recv_sem=recv_sem.at[b],
            device_id={"dom": dom_peer(offset)},
            device_id_type=MESH,
        )
        copy.start()
        copies.append(copy)
    return copies


def first_kernel(s, u, m, a, ghosts, total, gx, gy, gz, part, send_sem, recv_sem):
    greet(False)
    copies = start_sides(s, ghosts, send_sem, recv_sem)
    volume(u, m, a, gx, gy, gz, part)
    sum_shots(part, total)
    for copy in copies:
        copy.wait()


def second_kernel(
    s, u, m, earlier, a, ghosts, gradient, gx, gy, gz, part, mine, theirs, send_sem, recv_sem, grad_send, grad_recv
):
    greet(True)
    copies = start_sides(s, ghosts, send_sem, recv_sem)
    volume(u, m, a, gx, gy, gz, part)
    sum_shots(part, mine, earlier)
    me = lax.axis_index("shot")
    own = pl.ds(pl.multiple_of(me * QUARTER, 8), QUARTER)
    outgoing = []
    for step in range(1, N_SHOT):
        peer = lax.rem(me + step, N_SHOT)
        copy = pltpu.make_async_remote_copy(
            src_ref=mine.at[pl.ds(pl.multiple_of(peer * QUARTER, 8), QUARTER)],
            dst_ref=theirs.at[step - 1],
            send_sem=grad_send.at[step - 1],
            recv_sem=grad_recv.at[step - 1],
            device_id={"shot": peer},
            device_id_type=MESH,
        )
        copy.start()
        outgoing.append(copy)
    for copy in outgoing:
        copy.wait_recv()
    summed = mine[own, :] + theirs[0] + theirs[1] + theirs[2]
    gradient[own, :] = 0.005 * summed
    spread = []
    for step in range(1, N_SHOT):
        peer = lax.rem(me + step, N_SHOT)
        copy = pltpu.make_async_remote_copy(
            src_ref=gradient.at[own],
            dst_ref=gradient.at[own],
            send_sem=grad_send.at[2 + step],
            recv_sem=grad_recv.at[2 + step],
            device_id={"shot": peer},
            device_id_type=MESH,
        )
        copy.start()
        spread.append(copy)
    for copy in outgoing:
        copy.wait_send()
    for copy in spread:
        copy.wait()
    for copy in copies:
        copy.wait()


def correct_face(face, p, u, m, source, target, mirror, ext):
    axis = face // 2
    sign = -1.0 if face % 2 == 0 else 1.0
    velocity_scale, stress_scale = mirror
    for q in range(5):
        n = face_node(face, p, q)
        lam, mu, buoy = (m[rows(c, n), :] for c in range(3))
        speed = 5.0 * jnp.sqrt((lam + 2.0 * mu) * buoy)
        speed_v = speed * velocity_scale
        speed_s = speed * stress_scale
        kb = (5.0 * sign) * buoy * stress_scale
        signed = (5.0 * sign) * velocity_scale
        kl = lam * signed
        km = mu * signed
        jump = [ext(q, field) - u[rows(field, n), :] for field in range(9)]
        for b in range(3):
            place = rows(b, n)
            target[place, :] = source[place, :] + (kb * jump[SLOTS[b][axis]] + speed_v * jump[b])
        pressure = kl * jump[axis]
        for pair, (b, c) in enumerate(PAIRS):
            amount = speed_s * jump[3 + pair]
            if b == c:
                amount = amount + pressure
            if axis == b and axis == c:
                amount = amount + (km + km) * jump[axis]
            elif axis == b:
                amount = amount + km * jump[c]
            elif axis == c:
                amount = amount + km * jump[b]
            place = rows(3 + pair, n)
            target[place, :] = source[place, :] + amount


def surface(u, m, ghosts, codes, a, target, scratch):
    row, lane, half = iotas()
    d = lax.axis_index("dom")
    here = [(d - offset >= 0) & (d - offset < N_DOM) for offset, side in ROUTES]
    present = [jnp.where(h, 1, 0) for h in here]

    def copy_slab(i, carry):
        for field in range(9):
            place = rows(field, 25 * i, 25)
            target[place, :] = a[place, :]
        return carry

    lax.fori_loop(1, 4, copy_slab, 0)

    face_codes, odd = [], jnp.zeros((8, 128), F32)
    for face in range(6):
        low = jnp.broadcast_to(codes[0:1, 256 * face : 256 * face + 128], (8, 128))
        high = jnp.broadcast_to(codes[0:1, 256 * face + 128 : 256 * face + 256], (8, 128))
        code = jnp.where(half == 0, low, high)
        face_codes.append(code)
        usual = ((code >> 8) == (face ^ 1)) | (code >= 1664)
        if face < 4:
            usual = usual | ((code >> 5) == 48 + face)
        odd = odd + jnp.where(usual, 0.0, 1.0)
    general = jnp.sum(odd) > 0.0

    def scales(code):
        free = code == 1664
        return jnp.where(free, 0.0, 1.0), jnp.where(free, 2.0, 1.0)

    @pl.when(jnp.logical_not(general))
    def _():
        for face in range(6):
            code = face_codes[face]
            opposite = face ^ 1
            local = (code >> 8) == opposite
            index = code & 127
            same = ((code >> 7) & 1) == half
            ghost = ghost_index = None
            if face < 4:
                ghost = ((code >> 5) == 48 + face) & (jnp.broadcast_to(present[face], (8, 128)) == 1)
                ghost_index = [(code & 31) + 32 * c for c in range(4)]
            mirror = scales(code)

            def body(p, carry, face=face, opposite=opposite, local=local, index=index, same=same, ghost=ghost,
                     ghost_index=ghost_index, mirror=mirror):
                cache = {}

                def ext(q, field):
                    x = u[rows(field, face_node(opposite, p, q)), :]
                    value = jnp.where(same, pick(x, index), pick(other_half(x), index))
                    outside = 0.0
                    if ghost is not None:
                        block, t = divmod(9 * q + field, 8)
                        if (block, t // 4) not in cache:
                            if block not in cache:
                                g = ghosts[rows(face * BLOCKS + 6 * p + block, 0, nodes=1), :]
                                cache[block] = (g, other_half(g))
                            g, swapped = cache[block]
                            cache[block, t // 4] = jnp.where(half == t // 4, g, swapped)
                        outside = jnp.where(ghost, pick(cache[block, t // 4], ghost_index[t % 4]), 0.0)
                    return jnp.where(local, value, outside)

                correct_face(face, p, u, m, a if face < 2 else target, target, mirror, ext)
                return carry

            lax.fori_loop(0, 5, body, 0)

    @pl.when(general)
    def _():
        for face in range(6):
            code = face_codes[face]
            index = code & 127
            from_half = (code >> 7) & 1
            mirror = scales(code)

            def body(p, carry, face=face, code=code, index=index, from_half=from_half, mirror=mirror):
                def column_body(column, inner):
                    q = column // 9
                    field = column - 9 * q
                    value = jnp.zeros((8, 128), F32)
                    for g in range(6):
                        x = u[rows(field, face_node(g, p, q)), :]
                        found = jnp.where(from_half == half, pick(x, index), pick(other_half(x), index))
                        value = jnp.where((code >> 8) == g, found, value)
                    block = column // 8
                    t = column - 8 * block
                    upper = t // 4
                    for b in range(4):
                        x = ghosts[rows(b * BLOCKS + 6 * p + block, 0, nodes=1), :]
                        x = jnp.where(half == upper, x, other_half(x))
                        found = pick(x, (code & 31) + 32 * (t - 4 * upper))
                        mask = ((code >> 5) == 48 + b) & (jnp.broadcast_to(present[b], (8, 128)) == 1)
                        value = jnp.where(mask, found, value)
                    scratch[rows(column, 0, nodes=1), :] = value
                    return inner

                lax.fori_loop(0, 45, column_body, 0)

                def ext(q, field):
                    return scratch[rows(9 * q + field, 0, nodes=1), :]

                correct_face(face, p, u, m, a if face < 2 else target, target, mirror, ext)
                return carry

            lax.fori_loop(0, 5, body, 0)


def middle_kernel(u, m, ghosts, codes, a, lists, target, s, scratch):
    surface(u, m, ghosts, codes, a, target, scratch)
    pack_sides(target, lists, s)


def last_kernel(u, m, ghosts, codes, a, start, reduced, fw, ad, gradient, end, scratch, sems):
    surface(u, m, ghosts, codes, a, end, scratch)

    def average(group, carry):
        for n in range(25):
            place = rows(0, 25 * group + n)
            end[place, :] = 0.5 * start[place, :] + 0.5 * end[place, :]
        return carry

    lax.fori_loop(0, 45, average, 0)
    copies = state_copies(end, (fw, ad), sems, False)
    for copy in copies:
        copy.start()
    for c in range(3):
        gradient[c, :, :] = reduced[pl.ds(128 * c, 125), :]
    for copy in copies:
        copy.wait()


def vmem(count):
    return [pl.BlockSpec(memory_space=pltpu.VMEM)] * count


def shape(*dims):
    return jax.ShapeDtypeStruct(dims, F32)


def kept(*dims):
    return pltpu.VMEM(dims, F32)


def outer(*arrays):
    return [pltpu.with_memory_space_constraint(x, pltpu.HBM) for x in arrays]


def keep(*arrays):
    return [pltpu.with_memory_space_constraint(x, pltpu.VMEM) for x in arrays]


STATE = kept(9000, 128)
SIDES = kept(4 * SIDE_ROWS, 128)
VOLUME_SCRATCH = [
    pltpu.VMEM((6000, 128), F32),
    pltpu.VMEM((1200, 128), F32),
    pltpu.VMEM((1200, 128), F32),
    pltpu.VMEM((3000, 128), F32),
]
ANY = pl.BlockSpec(memory_space=pltpu.HBM)
GRANT = 20 << 20


def pack_call(counts, forward, adjoint, material, lists):
    return pl.pallas_call(
        pack_kernel,
        out_shape=(STATE, kept(3000, 128), SIDES),
        in_specs=[pl.BlockSpec(memory_space=pltpu.SMEM), ANY, ANY] + vmem(2),
        out_specs=tuple(vmem(3)),
        scratch_shapes=[pltpu.SemaphoreType.DMA((4,))],
        compiler_params=pltpu.CompilerParams(vmem_limit_bytes=GRANT),
        name="pack",
    )(counts, *outer(forward, adjoint), material, lists)


def first_call(sides, u, m):
    return pl.pallas_call(
        first_kernel,
        out_shape=(STATE, SIDES, kept(384, 256)),
        in_specs=vmem(3),
        out_specs=tuple(vmem(3)),
        scratch_shapes=VOLUME_SCRATCH + [pltpu.SemaphoreType.DMA((4,)), pltpu.SemaphoreType.DMA((4,))],
        compiler_params=pltpu.CompilerParams(collective_id=0, has_side_effects=True, vmem_limit_bytes=GRANT),
        name="first",
    )(*keep(sides, u, m))


def second_call(sides, u, m, earlier):
    return pl.pallas_call(
        second_kernel,
        out_shape=(STATE, SIDES, kept(384, 256)),
        in_specs=vmem(4),
        out_specs=tuple(vmem(3)),
        scratch_shapes=VOLUME_SCRATCH
        + [
            pltpu.VMEM((384, 256), F32),
            pltpu.VMEM((3, QUARTER, 256), F32),
            pltpu.SemaphoreType.DMA((4,)),
            pltpu.SemaphoreType.DMA((4,)),
            pltpu.SemaphoreType.DMA((6,)),
            pltpu.SemaphoreType.DMA((6,)),
        ],
        compiler_params=pltpu.CompilerParams(collective_id=1, has_side_effects=True, vmem_limit_bytes=GRANT),
        name="second",
    )(*keep(sides, u, m, earlier))


def middle_call(u, m, ghosts, codes, a, lists):
    return pl.pallas_call(
        middle_kernel,
        out_shape=(STATE, SIDES),
        in_specs=vmem(6),
        out_specs=tuple(vmem(2)),
        scratch_shapes=[pltpu.VMEM((360, 128), F32)],
        compiler_params=pltpu.CompilerParams(vmem_limit_bytes=GRANT),
        name="middle",
    )(*keep(u, m, ghosts), codes, *keep(a), lists)


def last_call(u, m, ghosts, codes, a, start, reduced):
    return pl.pallas_call(
        last_kernel,
        out_shape=(shape(1125, 2, 2, 128), shape(1125, 2, 2, 128), shape(3, 125, 256)),
        in_specs=vmem(7),
        out_specs=(ANY, ANY, vmem(1)[0]),
        scratch_shapes=[
            pltpu.VMEM((9000, 128), F32),
            pltpu.VMEM((360, 128), F32),
            pltpu.SemaphoreType.DMA((4,)),
        ],
        compiler_params=pltpu.CompilerParams(vmem_limit_bytes=GRANT),
        name="last",
    )(*keep(u, m, ghosts), codes, *keep(a, start, reduced))


def as_rows(x):
    return x.reshape(2, 9, 125, 2, 128).transpose(1, 2, 3, 0, 4).reshape(1125, 2, 2, 128)


def as_array(x):
    return x.reshape(9, 125, 2, 2, 128).transpose(3, 0, 1, 2, 4).reshape(2, 9, 125, 256)


def shards(forward, adjoint, material, counts, send_list, neighbours):
    lists = send_list
    u0, m, sides = pack_call(counts, as_rows(forward), as_rows(adjoint), material, lists)
    a1, ghosts, earlier = first_call(sides, u0, m)
    u1, sides2 = middle_call(u0, m, ghosts, neighbours, a1, lists)
    a2, ghosts2, reduced = second_call(sides2, u1, m, earlier)
    fw, ad, gradient = last_call(u1, m, ghosts2, neighbours, a2, u0, reduced)
    return as_array(fw), as_array(ad), gradient


def solution(mesh):
    placed = (
        P("shot", None, None, "dom"),
        P("shot", None, None, "dom"),
        P(None, None, "dom"),
        P("dom"),
        P("dom", None, None),
        P("dom", None),
    )
    return jax.shard_map(
        shards,
        mesh=mesh,
        in_specs=placed,
        out_specs=placed[:3],
        check_vma=False,
    )
```

```python
import functools

import jax
import jax.numpy as jnp
import numpy as np
from jax import lax
from jax.experimental import pallas as pl
from jax.experimental.pallas import tpu as pltpu
from jax.sharding import PartitionSpec as P

MESH = pl.DeviceIdType.MESH
PAIRS = ((0, 0), (1, 1), (2, 2), (1, 2), (0, 2), (0, 1))
SLOTS = ((3, 8, 7), (8, 4, 6), (7, 6, 5))
N_DOM = 64
N_SHOT = 4
BLOCKS = 30
SIDE_ROWS = 8 * BLOCKS
QUARTER = 96
ROUTES = ((4, 1), (-4, 0), (1, 3), (-1, 2))
F32 = jnp.float32


def derivative_matrix():
    points = np.array([-1.0, -np.sqrt(3.0 / 7.0), 0.0, np.sqrt(3.0 / 7.0), 1.0])
    weights = [1.0 / np.prod([points[a] - points[b] for b in range(5) if b != a]) for a in range(5)]
    matrix = np.zeros((5, 5))
    for a in range(5):
        for b in range(5):
            if a != b:
                matrix[a, b] = weights[b] / weights[a] / (points[a] - points[b])
        matrix[a, a] = -np.sum(matrix[a])
    return matrix


D = derivative_matrix()


def line_derivative(u):
    e0, o0 = u[0] + u[4], u[0] - u[4]
    e1, o1 = u[1] + u[3], u[1] - u[3]
    even = [
        float((D[a, 0] + D[a, 4]) / 2) * e0 + float((D[a, 1] + D[a, 3]) / 2) * e1 + float(D[a, 2]) * u[2]
        for a in (0, 1)
    ]
    odd = [float((D[a, 0] - D[a, 4]) / 2) * o0 + float((D[a, 1] - D[a, 3]) / 2) * o1 for a in (0, 1, 2)]
    return [odd[0] + even[0], odd[1] + even[1], odd[2], odd[1] - even[1], odd[0] - even[0]]


def rows(field, node, count=1, nodes=125):
    start = 8 * (nodes * field + node)
    if not isinstance(start, int):
        start = pl.multiple_of(start, 8)
    return pl.ds(start, 8 * count)


def face_node(face, p, q):
    fixed = 0 if face % 2 == 0 else 4
    if face < 2:
        return 25 * fixed + 5 * p + q
    if face < 4:
        return 25 * p + 5 * fixed + q
    return 25 * p + 5 * q + fixed


def iotas():
    row = lax.broadcasted_iota(jnp.int32, (8, 128), 0)
    lane = lax.broadcasted_iota(jnp.int32, (8, 128), 1)
    return row, lane, row // 4


def pick(x, index):
    return jnp.take_along_axis(x, index, axis=1, mode="promise_in_bounds")


def other_half(x):
    return pltpu.roll(x, 4, 0)


def pack_sides(u, lists, s):
    row, lane, half = iotas()
    group = half * 4 + lane // 32
    for side in range(4):
        listed = jnp.tile(jnp.broadcast_to(lists[0, side : side + 1, :], (8, 32)), (1, 4))
        index = listed & 127
        from_half = listed >> 7
        here = from_half == half
        listed_slot = listed < 256

        def body(p, carry, side=side, index=index, here=here, listed_slot=listed_slot):
            packed = None
            for column in range(45):
                q, field = divmod(column, 9)
                x = u[rows(field, face_node(side, p, q)), :]
                value = pick(x, index)
                value = jnp.where(here, value, other_half(value))
                t = column % 8
                packed = value if t == 0 else jnp.where(group == t, value, packed)
                if t == 7 or column == 44:
                    s[rows(side * BLOCKS + p * 6 + column // 8, 0, nodes=1), :] = jnp.where(listed_slot, packed, 0.0)
            return carry

        lax.fori_loop(0, 5, body, 0)


def state_copies(packed, arrays, sems, inward):
    view = packed.reshape(1125, 8, 128)
    copies = []
    for kind, array in enumerate(arrays):
        for h in range(2):
            inside, outside = view.at[:, pl.ds(4 * h + 2 * kind, 2), :], array.at[:, h]
            pair = (outside, inside) if inward else (inside, outside)
            copies.append(pltpu.make_async_copy(*pair, sems.at[2 * kind + h]))
    return copies


def pack_kernel(count, fw, ad, mat, lists, u, m, s, sems):
    row, lane, half = iotas()
    copies = state_copies(u, (fw, ad), sems, True)
    for copy in copies:
        copy.start()

    def per_kind(c, carry):
        for h in range(2):
            for block in range(16):
                size = 8 if block < 15 else 5
                x = 0.01 * mat[c, pl.ds(8 * block, size), pl.ds(128 * h, 128)]
                for ks in range(4):
                    m[pl.ds(c * 1000 + 64 * block + 4 * h + ks, size, stride=8), :] = x
        return carry

    lax.fori_loop(0, 3, per_kind, 0)
    for copy in copies:
        copy.wait()
    live = lane + 128 * half < count[0]

    def mask(group, carry):
        for n in range(25):
            place = rows(0, 25 * group + n)
            u[place, :] = jnp.where(live, u[place, :], 0.0)
        return carry

    lax.fori_loop(0, 45, mask, 0)
    pack_sides(u, lists, s)


X_FIELDS = (0, 1, 2, 3, 8, 7)
Y_FIELDS = (0, 1, 2, 8, 4, 6)
Z_FIELDS = (0, 1, 2, 7, 6, 5)


def volume(u, m, a, gx, gy, gz, part):
    def x_lines(j, carry):
        for slot, field in enumerate(X_FIELDS):
            lines = [u[rows(field, 25 * i + 5 * j, 5), :] for i in range(5)]
            for i, value in enumerate(line_derivative(lines)):
                gx[rows(slot, 25 * i + 5 * j, 5), :] = value
        return carry

    lax.fori_loop(0, 5, x_lines, 0)

    def slab(i, carry):
        for slot, field in enumerate(Y_FIELDS):
            lines = [u[rows(field, 25 * i + 5 * j, 5), :] for j in range(5)]
            for j, value in enumerate(line_derivative(lines)):
                gy[rows(slot, 5 * j, 5, nodes=25), :] = value
        for slot, field in enumerate(Z_FIELDS):
            for j in range(5):
                lines = [u[rows(field, 25 * i + 5 * j + k), :] for k in range(5)]
                for k, value in enumerate(line_derivative(lines)):
                    gz[rows(slot, 5 * j + k, nodes=25), :] = value

        def line(j, inner):
            for k in range(5):
                n = 25 * i + 5 * j + k
                x = [gx[rows(slot, n), :] for slot in range(6)]
                y = [gy[rows(slot, 5 * j + k, nodes=25), :] for slot in range(6)]
                z = [gz[rows(slot, 5 * j + k, nodes=25), :] for slot in range(6)]
                state = [u[rows(field, n), :] for field in range(9)]
                lam, mu, buoy = (m[rows(c, n), :] for c in range(3))
                divergence = x[0] + y[1] + z[2]
                sdiv = [x[3] + y[3] + z[3], x[4] + y[4] + z[4], x[5] + y[5] + z[5]]
                shear = [y[2] + z[1], x[2] + z[0], x[1] + y[0]]
                diagonal = [x[0], y[1], z[2]]
                pressure = lam * divergence
                twice = mu + mu
                for b in range(3):
                    a[rows(b, n), :] = state[b] + buoy * sdiv[b]
                    a[rows(3 + b, n), :] = state[3 + b] + (pressure + twice * diagonal[b])
                    a[rows(6 + b, n), :] = state[6 + b] + mu * shear[b]
                dual = [pltpu.roll(v, 6, 0) for v in state]
                part[rows(0, n), :] = divergence * (dual[3] + dual[4] + dual[5])
                normal = diagonal[0] * dual[3] + diagonal[1] * dual[4] + diagonal[2] * dual[5]
                tangent = shear[0] * dual[6] + shear[1] * dual[7] + shear[2] * dual[8]
                part[rows(1, n), :] = (normal + normal) + tangent
                part[rows(2, n), :] = sdiv[0] * dual[0] + sdiv[1] * dual[1] + sdiv[2] * dual[2]
            return inner

        lax.fori_loop(0, 5, line, 0)
        return carry

    lax.fori_loop(0, 5, slab, 0)


def sum_shots(part, total, earlier=None):
    for c in range(3):
        for block in range(16):
            size = 8 if block < 15 else 5
            for h in range(2):
                start = 1000 * c + 64 * block + 4 * h
                value = part[pl.ds(start, size, stride=8), :] + part[pl.ds(start + 1, size, stride=8), :]
                where = (pl.ds(128 * c + 8 * block, size), pl.ds(128 * h, 128))
                if earlier is not None:
                    value = value + earlier[where]
                if size < 8:
                    total[pl.ds(128 * c + 8 * block, 8), pl.ds(128 * h, 128)] = jnp.zeros((8, 128), F32)
                total[where] = value


def dom_peer(offset):
    d = lax.axis_index("dom")
    return lax.rem(d + offset + N_DOM, N_DOM)


def greet(shots):
    barrier = pltpu.get_barrier_semaphore()
    for offset, side in ROUTES:
        pl.semaphore_signal(barrier, inc=1, device_id={"dom": dom_peer(offset)}, device_id_type=MESH)
    if shots:
        me = lax.axis_index("shot")
        for step in range(1, N_SHOT):
            peer = lax.rem(me + step, N_SHOT)
            pl.semaphore_signal(barrier, inc=1, device_id={"shot": peer}, device_id_type=MESH)
    pl.semaphore_wait(barrier, 4 + (3 if shots else 0))


def start_sides(s, ghosts, send_sem, recv_sem):
    copies = []
    for b, (offset, side) in enumerate(ROUTES):
        copy = pltpu.make_async_remote_copy(
            src_ref=s.at[pl.ds(side * SIDE_ROWS, SIDE_ROWS)],
            dst_ref=ghosts.at[pl.ds(b * SIDE_ROWS, SIDE_ROWS)],
            send_sem=send_sem.at[b],
            recv_sem=recv_sem.at[b],
            device_id={"dom": dom_peer(offset)},
            device_id_type=MESH,
        )
        copy.start()
        copies.append(copy)
    return copies


def first_kernel(s, u, m, codes, a, ghosts, total, gx, gy, gz, part, send_sem, recv_sem):
    greet(False)
    copies = start_sides(s, ghosts, send_sem, recv_sem)
    volume(u, m, a, gx, gy, gz, part)
    sum_shots(part, total)
    for face in range(6):
        local_face(face, u, m, codes, a)
    for copy in copies:
        copy.wait()


def second_kernel(
    s, u, m, codes, earlier, a, ghosts, gradient, gx, gy, gz, part, mine, theirs, send_sem, recv_sem, grad_send, grad_recv
):
    greet(True)
    copies = start_sides(s, ghosts, send_sem, recv_sem)
    volume(u, m, a, gx, gy, gz, part)
    sum_shots(part, mine, earlier)
    me = lax.axis_index("shot")
    own = pl.ds(pl.multiple_of(me * QUARTER, 8), QUARTER)
    outgoing = []
    for step in range(1, N_SHOT):
        peer = lax.rem(me + step, N_SHOT)
        copy = pltpu.make_async_remote_copy(
            src_ref=mine.at[pl.ds(pl.multiple_of(peer * QUARTER, 8), QUARTER)],
            dst_ref=theirs.at[step - 1],
            send_sem=grad_send.at[step - 1],
            recv_sem=grad_recv.at[step - 1],
            device_id={"shot": peer},
            device_id_type=MESH,
        )
        copy.start()
        outgoing.append(copy)
    for face in range(4):
        local_face(face, u, m, codes, a)
    for copy in outgoing:
        copy.wait_recv()
    summed = mine[own, :] + theirs[0] + theirs[1] + theirs[2]
    gradient[own, :] = 0.005 * summed
    spread = []
    for step in range(1, N_SHOT):
        peer = lax.rem(me + step, N_SHOT)
        copy = pltpu.make_async_remote_copy(
            src_ref=gradient.at[own],
            dst_ref=gradient.at[own],
            send_sem=grad_send.at[2 + step],
            recv_sem=grad_recv.at[2 + step],
            device_id={"shot": peer},
            device_id_type=MESH,
        )
        copy.start()
        spread.append(copy)
    for face in range(4, 6):
        local_face(face, u, m, codes, a)
    for copy in outgoing:
        copy.wait_send()
    for copy in spread:
        copy.wait()
    for copy in copies:
        copy.wait()


def add_face(face, p, m, target, jump_of, mirror=None, weight=1.0):
    axis = face // 2
    sign = -1.0 if face % 2 == 0 else 1.0
    for q in range(5):
        n = face_node(face, p, q)
        lam, mu, buoy = (m[rows(c, n), :] for c in range(3))
        speed_v = speed_s = (5.0 * weight) * jnp.sqrt((lam + 2.0 * mu) * buoy)
        kb, kl, km = ((5.0 * weight * sign) * x for x in (buoy, lam, mu))
        if mirror is not None:
            speed_v, kl, km = (x * mirror[0] for x in (speed_v, kl, km))
            speed_s, kb = (x * mirror[1] for x in (speed_s, kb))
        jump = [jump_of(q, field) for field in range(9)]
        for b in range(3):
            place = rows(b, n)
            target[place, :] = target[place, :] + (kb * jump[SLOTS[b][axis]] + speed_v * jump[b])
        pressure = kl * jump[axis]
        for pair, (b, c) in enumerate(PAIRS):
            amount = speed_s * jump[3 + pair]
            if b == c:
                amount = amount + pressure
            if axis == b and axis == c:
                amount = amount + (km + km) * jump[axis]
            elif axis == b:
                amount = amount + km * jump[c]
            elif axis == c:
                amount = amount + km * jump[b]
            place = rows(3 + pair, n)
            target[place, :] = target[place, :] + amount


def face_code(codes, face, half):
    low = jnp.broadcast_to(codes[0:1, 256 * face : 256 * face + 128], (8, 128))
    high = jnp.broadcast_to(codes[0:1, 256 * face + 128 : 256 * face + 256], (8, 128))
    return jnp.where(half == 0, low, high)


def local_face(face, u, m, codes, target):
    row, lane, half = iotas()
    code = face_code(codes, face, half)
    local = (code >> 8) == (face ^ 1)
    index = code & 127
    same = ((code >> 7) & 1) == half
    free = code == 1664
    mirror = jnp.where(free, 0.0, 1.0), jnp.where(free, 2.0, 1.0)

    def body(p, carry):
        def jump_of(q, field):
            x = u[rows(field, face_node(face ^ 1, p, q)), :]
            value = jnp.where(same, pick(x, index), pick(other_half(x), index))
            return jnp.where(local, value, 0.0) - u[rows(field, face_node(face, p, q)), :]

        add_face(face, p, m, target, jump_of, mirror)
        return carry

    lax.fori_loop(0, 5, body, 0)


def other_exteriors(u, m, ghosts, codes, target, scratch, weight=1.0):
    row, lane, half = iotas()
    d = lax.axis_index("dom")
    present = [jnp.where((d - offset >= 0) & (d - offset < N_DOM), 1, 0) for offset, side in ROUTES]
    face_codes, odd = [], jnp.zeros((8, 128), F32)
    for face in range(6):
        code = face_code(codes, face, half)
        face_codes.append(code)
        usual = ((code >> 8) == (face ^ 1)) | (code >= 1664)
        if face < 4:
            usual = usual | ((code >> 5) == 48 + face)
        odd = odd + jnp.where(usual, 0.0, 1.0)
    general = jnp.sum(odd) > 0.0

    def ghost_mask(code, b):
        return ((code >> 5) == 48 + b) & (jnp.broadcast_to(present[b], (8, 128)) == 1)

    @pl.when(jnp.logical_not(general))
    def _():
        for face in range(4):
            code = face_codes[face]
            ghost = ghost_mask(code, face)
            index = [(code & 31) + 32 * c for c in range(4)]

            def body(p, carry, face=face, ghost=ghost, index=index):
                cache = {}

                def jump_of(q, field):
                    block, t = divmod(9 * q + field, 8)
                    if (block, t // 4) not in cache:
                        if block not in cache:
                            g = ghosts[rows(face * BLOCKS + 6 * p + block, 0, nodes=1), :]
                            cache[block] = (g, other_half(g))
                        g, swapped = cache[block]
                        cache[block, t // 4] = jnp.where(half == t // 4, g, swapped)
                    return jnp.where(ghost, pick(cache[block, t // 4], index[t % 4]), 0.0)

                add_face(face, p, m, target, jump_of, weight=weight)
                return carry

            lax.fori_loop(0, 5, body, 0)

    @pl.when(general)
    def _():
        for face in range(6):
            code = face_codes[face]
            index = code & 127
            same = ((code >> 7) & 1) == half

            def body(p, carry, face=face, code=code, index=index, same=same):
                def column_body(column, inner):
                    q = column // 9
                    field = column - 9 * q
                    value = jnp.zeros((8, 128), F32)
                    for g in range(6):
                        if g != face ^ 1:
                            x = u[rows(field, face_node(g, p, q)), :]
                            found = jnp.where(same, pick(x, index), pick(other_half(x), index))
                            value = jnp.where((code >> 8) == g, found, value)
                    block = column // 8
                    t = column - 8 * block
                    upper = t // 4
                    for b in range(4):
                        x = ghosts[rows(b * BLOCKS + 6 * p + block, 0, nodes=1), :]
                        x = jnp.where(half == upper, x, other_half(x))
                        found = pick(x, (code & 31) + 32 * (t - 4 * upper))
                        value = jnp.where(ghost_mask(code, b), found, value)
                    scratch[rows(column, 0, nodes=1), :] = value
                    return inner

                lax.fori_loop(0, 45, column_body, 0)

                def jump_of(q, field):
                    return scratch[rows(9 * q + field, 0, nodes=1), :]

                add_face(face, p, m, target, jump_of, weight=weight)
                return carry

            lax.fori_loop(0, 5, body, 0)


def middle_kernel(u, m, ghosts, codes, a, lists, target, s, scratch):
    other_exteriors(u, m, ghosts, codes, target, scratch)
    pack_sides(target, lists, s)


def last_kernel(u, m, ghosts, codes, a, start, reduced, fw, ad, gradient, end, scratch, sems):
    def average(group, carry):
        for n in range(25):
            place = rows(0, 25 * group + n)
            end[place, :] = 0.5 * start[place, :] + 0.5 * a[place, :]
        return carry

    lax.fori_loop(0, 45, average, 0)
    other_exteriors(u, m, ghosts, codes, end, scratch, 0.5)
    copies = state_copies(end, (fw, ad), sems, False)
    for copy in copies:
        copy.start()
    for c in range(3):
        gradient[c, :, :] = reduced[pl.ds(128 * c, 125), :]
    for copy in copies:
        copy.wait()


def vmem(count):
    return [pl.BlockSpec(memory_space=pltpu.VMEM)] * count


def shape(*dims):
    return jax.ShapeDtypeStruct(dims, F32)


def kept(*dims):
    return pltpu.VMEM(dims, F32)


def outer(*arrays):
    return [pltpu.with_memory_space_constraint(x, pltpu.HBM) for x in arrays]


def keep(*arrays):
    return [pltpu.with_memory_space_constraint(x, pltpu.VMEM) for x in arrays]


STATE = kept(9000, 128)
SIDES = kept(4 * SIDE_ROWS, 128)
VOLUME_SCRATCH = [
    pltpu.VMEM((6000, 128), F32),
    pltpu.VMEM((1200, 128), F32),
    pltpu.VMEM((1200, 128), F32),
    pltpu.VMEM((3000, 128), F32),
]
ANY = pl.BlockSpec(memory_space=pltpu.HBM)
GRANT = 20 << 20


def pack_call(counts, forward, adjoint, material, lists):
    return pl.pallas_call(
        pack_kernel,
        out_shape=(STATE, kept(3000, 128), SIDES),
        in_specs=[pl.BlockSpec(memory_space=pltpu.SMEM), ANY, ANY] + vmem(2),
        out_specs=tuple(vmem(3)),
        scratch_shapes=[pltpu.SemaphoreType.DMA((4,))],
        compiler_params=pltpu.CompilerParams(vmem_limit_bytes=GRANT),
        name="pack",
    )(counts, *outer(forward, adjoint), material, lists)


def first_call(sides, u, m, codes):
    return pl.pallas_call(
        first_kernel,
        out_shape=(STATE, SIDES, kept(384, 256)),
        in_specs=vmem(4),
        out_specs=tuple(vmem(3)),
        scratch_shapes=VOLUME_SCRATCH + [pltpu.SemaphoreType.DMA((4,)), pltpu.SemaphoreType.DMA((4,))],
        compiler_params=pltpu.CompilerParams(collective_id=0, has_side_effects=True, vmem_limit_bytes=GRANT),
        name="first",
    )(*keep(sides, u, m), codes)


def second_call(sides, u, m, codes, earlier):
    return pl.pallas_call(
        second_kernel,
        out_shape=(STATE, SIDES, kept(384, 256)),
        in_specs=vmem(5),
        out_specs=tuple(vmem(3)),
        scratch_shapes=VOLUME_SCRATCH
        + [
            pltpu.VMEM((384, 256), F32),
            pltpu.VMEM((3, QUARTER, 256), F32),
            pltpu.SemaphoreType.DMA((4,)),
            pltpu.SemaphoreType.DMA((4,)),
            pltpu.SemaphoreType.DMA((6,)),
            pltpu.SemaphoreType.DMA((6,)),
        ],
        compiler_params=pltpu.CompilerParams(collective_id=1, has_side_effects=True, vmem_limit_bytes=GRANT),
        name="second",
    )(*keep(sides, u, m), codes, *keep(earlier))


def middle_call(u, m, ghosts, codes, a, lists):
    return pl.pallas_call(
        middle_kernel,
        out_shape=(STATE, SIDES),
        in_specs=vmem(6),
        out_specs=tuple(vmem(2)),
        scratch_shapes=[pltpu.VMEM((360, 128), F32)],
        input_output_aliases={4: 0},
        compiler_params=pltpu.CompilerParams(vmem_limit_bytes=GRANT),
        name="middle",
    )(*keep(u, m, ghosts), codes, *keep(a), lists)


def last_call(u, m, ghosts, codes, a, start, reduced):
    return pl.pallas_call(
        last_kernel,
        out_shape=(shape(1125, 2, 2, 128), shape(1125, 2, 2, 128), shape(3, 125, 256)),
        in_specs=vmem(7),
        out_specs=(ANY, ANY, vmem(1)[0]),
        scratch_shapes=[
            pltpu.VMEM((9000, 128), F32),
            pltpu.VMEM((360, 128), F32),
            pltpu.SemaphoreType.DMA((4,)),
        ],
        compiler_params=pltpu.CompilerParams(vmem_limit_bytes=GRANT),
        name="last",
    )(*keep(u, m, ghosts), codes, *keep(a, start, reduced))


def as_rows(x):
    return x.reshape(2, 9, 125, 2, 128).transpose(1, 2, 3, 0, 4).reshape(1125, 2, 2, 128)


def as_array(x):
    return x.reshape(9, 125, 2, 2, 128).transpose(3, 0, 1, 2, 4).reshape(2, 9, 125, 256)


def shards(forward, adjoint, material, counts, send_list, neighbours):
    lists = send_list
    u0, m, sides = pack_call(counts, as_rows(forward), as_rows(adjoint), material, lists)
    a1, ghosts, earlier = first_call(sides, u0, m, neighbours)
    u1, sides2 = middle_call(u0, m, ghosts, neighbours, a1, lists)
    a2, ghosts2, reduced = second_call(sides2, u1, m, neighbours, earlier)
    fw, ad, gradient = last_call(u1, m, ghosts2, neighbours, a2, u0, reduced)
    return as_array(fw), as_array(ad), gradient


def solution(mesh):
    placed = (
        P("shot", None, None, "dom"),
        P("shot", None, None, "dom"),
        P(None, None, "dom"),
        P("dom"),
        P("dom", None, None),
        P("dom", None),
    )
    return jax.shard_map(
        shards,
        mesh=mesh,
        in_specs=placed,
        out_specs=placed[:3],
        check_vma=False,
    )
```

```python
import functools

import jax
import jax.numpy as jnp
import numpy as np
from jax import lax
from jax.experimental import pallas as pl
from jax.experimental.pallas import tpu as pltpu
from jax.sharding import PartitionSpec as P

MESH = pl.DeviceIdType.MESH
PAIRS = ((0, 0), (1, 1), (2, 2), (1, 2), (0, 2), (0, 1))
SLOTS = ((3, 8, 7), (8, 4, 6), (7, 6, 5))
N_DOM = 64
N_SHOT = 4
BLOCKS = 30
SIDE_ROWS = 8 * BLOCKS
QUARTER = 96
ROUTES = ((4, 1), (-4, 0), (1, 3), (-1, 2))
F32 = jnp.float32


def derivative_matrix():
    points = np.array([-1.0, -np.sqrt(3.0 / 7.0), 0.0, np.sqrt(3.0 / 7.0), 1.0])
    weights = [1.0 / np.prod([points[a] - points[b] for b in range(5) if b != a]) for a in range(5)]
    matrix = np.zeros((5, 5))
    for a in range(5):
        for b in range(5):
            if a != b:
                matrix[a, b] = weights[b] / weights[a] / (points[a] - points[b])
        matrix[a, a] = -np.sum(matrix[a])
    return matrix


D = derivative_matrix()


def line_derivative(u):
    e0, o0 = u[0] + u[4], u[0] - u[4]
    e1, o1 = u[1] + u[3], u[1] - u[3]
    even = [
        float((D[a, 0] + D[a, 4]) / 2) * e0 + float((D[a, 1] + D[a, 3]) / 2) * e1 + float(D[a, 2]) * u[2]
        for a in (0, 1)
    ]
    odd = [float((D[a, 0] - D[a, 4]) / 2) * o0 + float((D[a, 1] - D[a, 3]) / 2) * o1 for a in (0, 1, 2)]
    return [odd[0] + even[0], odd[1] + even[1], odd[2], odd[1] - even[1], odd[0] - even[0]]


def rows(field, node, count=1, nodes=125):
    start = 8 * (nodes * field + node)
    if not isinstance(start, int):
        start = pl.multiple_of(start, 8)
    return pl.ds(start, 8 * count)


def face_node(face, p, q):
    fixed = 0 if face % 2 == 0 else 4
    if face < 2:
        return 25 * fixed + 5 * p + q
    if face < 4:
        return 25 * p + 5 * fixed + q
    return 25 * p + 5 * q + fixed


def iotas():
    row = lax.broadcasted_iota(jnp.int32, (8, 128), 0)
    lane = lax.broadcasted_iota(jnp.int32, (8, 128), 1)
    return row, lane, row // 4


def pick(x, index):
    return jnp.take_along_axis(x, index, axis=1, mode="promise_in_bounds")


def other_half(x):
    return pltpu.roll(x, 4, 0)


def pack_sides(u, lists, s):
    row, lane, half = iotas()
    group = half * 4 + lane // 32
    sides = []
    for side in range(4):
        listed = jnp.tile(jnp.broadcast_to(lists[0, side : side + 1, :], (8, 32)), (1, 4))
        sides.append((listed & 127, (listed >> 7) == half, listed < 256))

    def body(p, carry):
        for side, (index, here, listed_slot) in enumerate(sides):
            packed = None
            for column in range(45):
                q, field = divmod(column, 9)
                x = u[rows(field, face_node(side, p, q)), :]
                value = pick(x, index)
                value = jnp.where(here, value, other_half(value))
                t = column % 8
                packed = value if t == 0 else jnp.where(group == t, value, packed)
                if t == 7 or column == 44:
                    s[rows(side * BLOCKS + p * 6 + column // 8, 0, nodes=1), :] = jnp.where(listed_slot, packed, 0.0)
        return carry

    lax.fori_loop(0, 5, body, 0)


def state_copies(packed, arrays, sems, inward):
    view = packed.reshape(1125, 8, 128)
    copies = []
    for kind, array in enumerate(arrays):
        for h in range(2):
            inside, outside = view.at[:, pl.ds(4 * h + 2 * kind, 2), :], array.at[:, h]
            pair = (outside, inside) if inward else (inside, outside)
            copies.append(pltpu.make_async_copy(*pair, sems.at[2 * kind + h]))
    return copies


X_FIELDS = (0, 1, 2, 3, 8, 7)
Y_FIELDS = (0, 1, 2, 8, 4, 6)
Z_FIELDS = (0, 1, 2, 7, 6, 5)


def volume(u, m, codes, a, gx, gy, gz, part, with_faces):
    x_faces = local_faces(codes, (0, 1), u) if with_faces else None

    def x_lines(j, carry):
        for slot, field in enumerate(X_FIELDS):
            lines = [u[rows(field, 25 * i + 5 * j, 5), :] for i in range(5)]
            for i, value in enumerate(line_derivative(lines)):
                gx[rows(slot, 25 * i + 5 * j, 5), :] = value
        if not with_faces:
            return carry
        for face in (0, 1):
            jumps, mirror = x_faces[face]
            for q in range(5):
                n = face_node(face, j, q)
                medium = [m[rows(c, n), :] for c in range(3)]
                own = [u[rows(field, n), :] for field in range(9)]
                amounts = corrections(face, jumps(j, q, own), medium, wave_speed(medium), mirror)
                for field in range(9):
                    a[rows(field, n), :] = own[field] + amounts[field]
        for i in (1, 2, 3):
            for field in range(9):
                place = rows(field, 25 * i + 5 * j, 5)
                a[place, :] = u[place, :]
        return carry

    lax.fori_loop(0, 5, x_lines, 0)
    other_faces = local_faces(codes, (2, 3, 4, 5), u) if with_faces else None

    def slab(i, carry):
        for slot, field in enumerate(Y_FIELDS):
            lines = [u[rows(field, 25 * i + 5 * j, 5), :] for j in range(5)]
            for j, value in enumerate(line_derivative(lines)):
                gy[rows(slot, 5 * j, 5, nodes=25), :] = value
        for slot, field in enumerate(Z_FIELDS):
            for j in range(5):
                lines = [u[rows(field, 25 * i + 5 * j + k), :] for k in range(5)]
                for k, value in enumerate(line_derivative(lines)):
                    gz[rows(slot, 5 * j + k, nodes=25), :] = value
        for j in range(5):
            for k in range(5):
                n = 25 * i + 5 * j + k
                x = [gx[rows(slot, n), :] for slot in range(6)]
                y = [gy[rows(slot, 5 * j + k, nodes=25), :] for slot in range(6)]
                z = [gz[rows(slot, 5 * j + k, nodes=25), :] for slot in range(6)]
                state = [u[rows(field, n), :] for field in range(9)]
                out = [a[rows(field, n), :] for field in range(9)] if with_faces else list(state)
                medium = lam, mu, buoy = [m[rows(c, n), :] for c in range(3)]
                divergence = x[0] + y[1] + z[2]
                sdiv = [x[3] + y[3] + z[3], x[4] + y[4] + z[4], x[5] + y[5] + z[5]]
                shear = [y[2] + z[1], x[2] + z[0], x[1] + y[0]]
                diagonal = [x[0], y[1], z[2]]
                pressure = lam * divergence
                twice = mu + mu
                for b in range(3):
                    out[b] = out[b] + buoy * sdiv[b]
                    out[3 + b] = out[3 + b] + (pressure + twice * diagonal[b])
                    out[6 + b] = out[6 + b] + mu * shear[b]
                touching = [(face, q) for face, at, q in ((2, j == 0, k), (3, j == 4, k), (4, k == 0, j), (5, k == 4, j)) if at]
                if with_faces and touching:
                    speed = wave_speed(medium)
                    for face, q in touching:
                        jumps, mirror = other_faces[face]
                        amounts = corrections(face, jumps(i, q, state), medium, speed, mirror)
                        out = [x + y for x, y in zip(out, amounts)]
                for field in range(9):
                    a[rows(field, n), :] = out[field]
                dual = [pltpu.roll(v, 6, 0) for v in state]
                part[rows(0, n), :] = divergence * (dual[3] + dual[4] + dual[5])
                normal = diagonal[0] * dual[3] + diagonal[1] * dual[4] + diagonal[2] * dual[5]
                tangent = shear[0] * dual[6] + shear[1] * dual[7] + shear[2] * dual[8]
                part[rows(1, n), :] = (normal + normal) + tangent
                part[rows(2, n), :] = sdiv[0] * dual[0] + sdiv[1] * dual[1] + sdiv[2] * dual[2]
        return carry

    lax.fori_loop(0, 5, slab, 0)


def sum_shots(part, total, earlier=None):
    for c in range(3):
        for block in range(16):
            size = 8 if block < 15 else 5
            for h in range(2):
                start = 1000 * c + 64 * block + 4 * h
                value = part[pl.ds(start, size, stride=8), :] + part[pl.ds(start + 1, size, stride=8), :]
                where = (pl.ds(128 * c + 8 * block, size), pl.ds(128 * h, 128))
                if earlier is not None:
                    value = value + earlier[where]
                if size < 8:
                    total[pl.ds(128 * c + 8 * block, 8), pl.ds(128 * h, 128)] = jnp.zeros((8, 128), F32)
                total[where] = value


def dom_peer(offset):
    d = lax.axis_index("dom")
    return lax.rem(d + offset + N_DOM, N_DOM)


def greet(shots):
    barrier = pltpu.get_barrier_semaphore()
    for offset, side in ROUTES:
        pl.semaphore_signal(barrier, inc=1, device_id={"dom": dom_peer(offset)}, device_id_type=MESH)
    if shots:
        me = lax.axis_index("shot")
        for step in range(1, N_SHOT):
            peer = lax.rem(me + step, N_SHOT)
            pl.semaphore_signal(barrier, inc=1, device_id={"shot": peer}, device_id_type=MESH)


def greeted(shots):
    pl.semaphore_wait(pltpu.get_barrier_semaphore(), 4 + (3 if shots else 0))


def start_sides(s, ghosts, send_sem, recv_sem):
    copies = []
    for b, (offset, side) in enumerate(ROUTES):
        copy = pltpu.make_async_remote_copy(
            src_ref=s.at[pl.ds(side * SIDE_ROWS, SIDE_ROWS)],
            dst_ref=ghosts.at[pl.ds(b * SIDE_ROWS, SIDE_ROWS)],
            send_sem=send_sem.at[b],
            recv_sem=recv_sem.at[b],
            device_id={"dom": dom_peer(offset)},
            device_id_type=MESH,
        )
        copy.start()
        copies.append(copy)
    return copies


def first_kernel(
    count, fw, ad, mat, lists, codes, u, m, a, ghosts, total, s, gx, gy, gz, part, send_sem, recv_sem, sems
):
    greet(False)
    row, lane, half = iotas()
    copies = state_copies(u, (fw, ad), sems, True)
    for copy in copies:
        copy.start()

    def per_kind(c, carry):
        for h in range(2):
            for block in range(16):
                size = 8 if block < 15 else 5
                x = 0.01 * mat[c, pl.ds(8 * block, size), pl.ds(128 * h, 128)]
                for ks in range(4):
                    m[pl.ds(c * 1000 + 64 * block + 4 * h + ks, size, stride=8), :] = x
        return carry

    lax.fori_loop(0, 3, per_kind, 0)
    for copy in copies:
        copy.wait()
    live = lane + 128 * half < count[0]

    def mask(group, carry):
        for n in range(25):
            place = rows(0, 25 * group + n)
            u[place, :] = jnp.where(live, u[place, :], 0.0)
        return carry

    lax.fori_loop(0, 45, mask, 0)
    pack_sides(u, lists, s)
    greeted(False)
    copies = start_sides(s, ghosts, send_sem, recv_sem)
    volume(u, m, codes, a, gx, gy, gz, part, True)
    sum_shots(part, total)
    for copy in copies:
        copy.wait()


def second_kernel(
    u, m, codes, lists, earlier, a, ghosts, gradient, s, gx, gy, gz, part, mine, theirs,
    send_sem, recv_sem, reduce_send, reduce_recv, spread_send, spread_recv,
):
    greet(True)
    pack_sides(u, lists, s)
    greeted(True)
    copies = start_sides(s, ghosts, send_sem, recv_sem)
    volume(u, m, codes, a, gx, gy, gz, part, False)
    sum_shots(part, mine, earlier)
    me = lax.axis_index("shot")

    def piece(owner):
        return pl.ds(pl.multiple_of(QUARTER * owner, 8), QUARTER)

    def exchange(source, target, sends, receives, step):
        return pltpu.make_async_remote_copy(
            src_ref=source,
            dst_ref=target,
            send_sem=sends.at[step - 1],
            recv_sem=receives.at[step - 1],
            device_id={"shot": lax.rem(me + step, N_SHOT)},
            device_id_type=MESH,
        )

    outgoing = [
        exchange(mine.at[piece(lax.rem(me + step, N_SHOT))], theirs.at[step - 1], reduce_send, reduce_recv, step)
        for step in (2, 1, 3)
    ]
    for copy in outgoing:
        copy.start()
    add_local_faces((0, 1), u, m, codes, a)
    add_local_faces((2, 3), u, m, codes, a)
    for copy in outgoing:
        copy.wait_recv()
    own = piece(me)
    gradient[own, :] = 0.005 * (mine[own, :] + theirs[0] + theirs[1] + theirs[2])
    spread = [exchange(gradient.at[own], gradient.at[own], spread_send, spread_recv, step) for step in (2, 1, 3)]
    for copy in spread:
        copy.start()
    add_local_faces((4, 5), u, m, codes, a)
    for copy in outgoing:
        copy.wait_send()
    for copy in spread:
        copy.wait()
    for copy in copies:
        copy.wait()


def corrections(face, jump, medium, speed, mirror=None, weight=1.0):
    axis = face // 2
    sign = -1.0 if face % 2 == 0 else 1.0
    lam, mu, buoy = medium
    speed_v = speed_s = speed if weight == 1.0 else weight * speed
    kb, kl, km = ((5.0 * weight * sign) * x for x in (buoy, lam, mu))
    if mirror is not None:
        speed_v, kl, km = (x * mirror[0] for x in (speed_v, kl, km))
        speed_s, kb = (x * mirror[1] for x in (speed_s, kb))
    out = [kb * jump[SLOTS[b][axis]] + speed_v * jump[b] for b in range(3)]
    pressure = kl * jump[axis]
    for pair, (b, c) in enumerate(PAIRS):
        amount = speed_s * jump[3 + pair]
        if b == c:
            amount = amount + pressure
        if axis == b and axis == c:
            amount = amount + (km + km) * jump[axis]
        elif axis == b:
            amount = amount + km * jump[c]
        elif axis == c:
            amount = amount + km * jump[b]
        out.append(amount)
    return out


def wave_speed(medium):
    lam, mu, buoy = medium
    return 5.0 * jnp.sqrt((lam + 2.0 * mu) * buoy)


def add_face(face, p, m, target, jump_of, weight=1.0):
    for q in range(5):
        n = face_node(face, p, q)
        medium = [m[rows(c, n), :] for c in range(3)]
        jump = [jump_of(q, field) for field in range(9)]
        for field, amount in enumerate(corrections(face, jump, medium, wave_speed(medium), weight=weight)):
            place = rows(field, n)
            target[place, :] = target[place, :] + amount


def face_code(codes, face, half):
    low = jnp.broadcast_to(codes[0:1, 256 * face : 256 * face + 128], (8, 128))
    high = jnp.broadcast_to(codes[0:1, 256 * face + 128 : 256 * face + 256], (8, 128))
    return jnp.where(half == 0, low, high)


def local_faces(codes, faces, u):
    row, lane, half = iotas()
    found = {}
    for face in faces:
        code = face_code(codes, face, half)
        local = (code >> 8) == (face ^ 1)
        index = code & 127
        same = ((code >> 7) & 1) == half
        free = code == 1664
        mirror = jnp.where(free, 0.0, 1.0), jnp.where(free, 2.0, 1.0)

        def jumps(p, q, own, face=face, local=local, index=index, same=same):
            out = []
            for field in range(9):
                x = u[rows(field, face_node(face ^ 1, p, q)), :]
                value = jnp.where(same, pick(x, index), pick(other_half(x), index))
                out.append(jnp.where(local, value, 0.0) - own[field])
            return out

        found[face] = (jumps, mirror)
    return found


def add_local_faces(faces, u, m, codes, target):
    found = local_faces(codes, faces, u)

    def body(p, carry):
        for face in faces:
            jumps, mirror = found[face]
            for q in range(5):
                n = face_node(face, p, q)
                medium = [m[rows(c, n), :] for c in range(3)]
                own = [u[rows(field, n), :] for field in range(9)]
                amounts = corrections(face, jumps(p, q, own), medium, wave_speed(medium), mirror)
                for field, amount in enumerate(amounts):
                    place = rows(field, n)
                    target[place, :] = target[place, :] + amount
        return carry

    lax.fori_loop(0, 5, body, 0)


def other_exteriors(u, m, ghosts, codes, target, scratch, weight=1.0):
    row, lane, half = iotas()
    d = lax.axis_index("dom")
    present = [jnp.where((d - offset >= 0) & (d - offset < N_DOM), 1, 0) for offset, side in ROUTES]
    face_codes, odd = [], jnp.zeros((8, 128), F32)
    for face in range(6):
        code = face_code(codes, face, half)
        face_codes.append(code)
        usual = ((code >> 8) == (face ^ 1)) | (code >= 1664)
        if face < 4:
            usual = usual | ((code >> 5) == 48 + face)
        odd = odd + jnp.where(usual, 0.0, 1.0)
    general = jnp.sum(odd) > 0.0

    def ghost_mask(code, b):
        return ((code >> 5) == 48 + b) & (jnp.broadcast_to(present[b], (8, 128)) == 1)

    @pl.when(jnp.logical_not(general))
    def _():
        sides = []
        for face in range(4):
            code = face_codes[face]
            sides.append((ghost_mask(code, face), [(code & 31) + 32 * c for c in range(4)]))

        def body(p, carry):
            for face, (ghost, index) in enumerate(sides):
                cache = {}

                def jump_of(q, field):
                    block, t = divmod(9 * q + field, 8)
                    if (block, t // 4) not in cache:
                        if block not in cache:
                            g = ghosts[rows(face * BLOCKS + 6 * p + block, 0, nodes=1), :]
                            cache[block] = (g, other_half(g))
                        g, swapped = cache[block]
                        cache[block, t // 4] = jnp.where(half == t // 4, g, swapped)
                    return jnp.where(ghost, pick(cache[block, t // 4], index[t % 4]), 0.0)

                add_face(face, p, m, target, jump_of, weight=weight)
            return carry

        lax.fori_loop(0, 5, body, 0)

    @pl.when(general)
    def _():
        for face in range(6):
            code = face_codes[face]
            index = code & 127
            same = ((code >> 7) & 1) == half

            def body(p, carry, face=face, code=code, index=index, same=same):
                def column_body(column, inner):
                    q = column // 9
                    field = column - 9 * q
                    value = jnp.zeros((8, 128), F32)
                    for g in range(6):
                        if g != face ^ 1:
                            x = u[rows(field, face_node(g, p, q)), :]
                            found = jnp.where(same, pick(x, index), pick(other_half(x), index))
                            value = jnp.where((code >> 8) == g, found, value)
                    block = column // 8
                    t = column - 8 * block
                    upper = t // 4
                    for b in range(4):
                        x = ghosts[rows(b * BLOCKS + 6 * p + block, 0, nodes=1), :]
                        x = jnp.where(half == upper, x, other_half(x))
                        found = pick(x, (code & 31) + 32 * (t - 4 * upper))
                        value = jnp.where(ghost_mask(code, b), found, value)
                    scratch[rows(column, 0, nodes=1), :] = value
                    return inner

                lax.fori_loop(0, 45, column_body, 0)

                def jump_of(q, field):
                    return scratch[rows(9 * q + field, 0, nodes=1), :]

                add_face(face, p, m, target, jump_of, weight=weight)
                return carry

            lax.fori_loop(0, 5, body, 0)


def middle_kernel(u, m, ghosts, codes, a, target, scratch):
    other_exteriors(u, m, ghosts, codes, target, scratch)


def last_kernel(u, m, ghosts, codes, a, start, reduced, fw, ad, gradient, end, scratch, sems):
    def average(group, carry):
        for n in range(25):
            place = rows(0, 25 * group + n)
            end[place, :] = 0.5 * start[place, :] + 0.5 * a[place, :]
        return carry

    lax.fori_loop(0, 45, average, 0)
    other_exteriors(u, m, ghosts, codes, end, scratch, 0.5)
    copies = state_copies(end, (fw, ad), sems, False)
    for copy in copies:
        copy.start()
    for c in range(3):
        gradient[c, :, :] = reduced[pl.ds(128 * c, 125), :]
    for copy in copies:
        copy.wait()


def vmem(count):
    return [pl.BlockSpec(memory_space=pltpu.VMEM)] * count


def shape(*dims):
    return jax.ShapeDtypeStruct(dims, F32)


def kept(*dims):
    return pltpu.VMEM(dims, F32)


def outer(*arrays):
    return [pltpu.with_memory_space_constraint(x, pltpu.HBM) for x in arrays]


def keep(*arrays):
    return [pltpu.with_memory_space_constraint(x, pltpu.VMEM) for x in arrays]


STATE = kept(9000, 128)
SIDES = kept(4 * SIDE_ROWS, 128)
TOTALS = kept(384, 256)
VOLUME_SCRATCH = [SIDES, kept(6000, 128), kept(1200, 128), kept(1200, 128), kept(3000, 128)]
HBM = pl.BlockSpec(memory_space=pltpu.HBM)
GRANT = 20 << 20


def copies_semaphore(count):
    return pltpu.SemaphoreType.DMA((count,))


def first_call(counts, forward, adjoint, material, lists, codes):
    return pl.pallas_call(
        first_kernel,
        out_shape=(STATE, kept(3000, 128), STATE, SIDES, TOTALS),
        in_specs=[pl.BlockSpec(memory_space=pltpu.SMEM), HBM, HBM] + vmem(3),
        out_specs=tuple(vmem(5)),
        scratch_shapes=VOLUME_SCRATCH + [copies_semaphore(4)] * 3,
        compiler_params=pltpu.CompilerParams(collective_id=0, has_side_effects=True, vmem_limit_bytes=GRANT),
        name="first",
    )(counts, *outer(forward, adjoint), material, lists, codes)


def second_call(u, m, codes, lists, earlier):
    return pl.pallas_call(
        second_kernel,
        out_shape=(STATE, SIDES, TOTALS),
        in_specs=vmem(5),
        out_specs=tuple(vmem(3)),
        scratch_shapes=VOLUME_SCRATCH
        + [TOTALS, kept(3, QUARTER, 256)]
        + [copies_semaphore(4)] * 2
        + [copies_semaphore(3)] * 4,
        compiler_params=pltpu.CompilerParams(collective_id=1, has_side_effects=True, vmem_limit_bytes=GRANT),
        name="second",
    )(*keep(u, m), codes, lists, *keep(earlier))


def middle_call(u, m, ghosts, codes, a):
    return pl.pallas_call(
        middle_kernel,
        out_shape=STATE,
        in_specs=vmem(5),
        out_specs=vmem(1)[0],
        scratch_shapes=[pltpu.VMEM((360, 128), F32)],
        input_output_aliases={4: 0},
        compiler_params=pltpu.CompilerParams(vmem_limit_bytes=GRANT),
        name="middle",
    )(*keep(u, m, ghosts), codes, *keep(a))


def last_call(u, m, ghosts, codes, a, start, reduced):
    return pl.pallas_call(
        last_kernel,
        out_shape=(shape(1125, 2, 2, 128), shape(1125, 2, 2, 128), shape(3, 125, 256)),
        in_specs=vmem(7),
        out_specs=(HBM, HBM, vmem(1)[0]),
        scratch_shapes=[
            pltpu.VMEM((9000, 128), F32),
            pltpu.VMEM((360, 128), F32),
            pltpu.SemaphoreType.DMA((4,)),
        ],
        compiler_params=pltpu.CompilerParams(vmem_limit_bytes=GRANT),
        name="last",
    )(*keep(u, m, ghosts), codes, *keep(a, start, reduced))


def as_rows(x):
    return x.reshape(2, 9, 125, 2, 128).transpose(1, 2, 3, 0, 4).reshape(1125, 2, 2, 128)


def as_array(x):
    return x.reshape(9, 125, 2, 2, 128).transpose(3, 0, 1, 2, 4).reshape(2, 9, 125, 256)


def shards(forward, adjoint, material, counts, send_list, neighbours):
    u0, m, a1, ghosts, earlier = first_call(
        counts, as_rows(forward), as_rows(adjoint), material, send_list, neighbours
    )
    u1 = middle_call(u0, m, ghosts, neighbours, a1)
    a2, ghosts2, reduced = second_call(u1, m, neighbours, send_list, earlier)
    fw, ad, gradient = last_call(u1, m, ghosts2, neighbours, a2, u0, reduced)
    return as_array(fw), as_array(ad), gradient


def solution(mesh):
    placed = (
        P("shot", None, None, "dom"),
        P("shot", None, None, "dom"),
        P(None, None, "dom"),
        P("dom"),
        P("dom", None, None),
        P("dom", None),
    )
    return jax.shard_map(
        shards,
        mesh=mesh,
        in_specs=placed,
        out_specs=placed[:3],
        check_vma=False,
    )
```

```python
import functools

import jax
import jax.numpy as jnp
import numpy as np
from jax import lax
from jax.experimental import pallas as pl
from jax.experimental.pallas import tpu as pltpu
from jax.sharding import PartitionSpec as P

MESH = pl.DeviceIdType.MESH
PAIRS = ((0, 0), (1, 1), (2, 2), (1, 2), (0, 2), (0, 1))
SLOTS = ((3, 8, 7), (8, 4, 6), (7, 6, 5))
N_DOM = 64
N_SHOT = 4
BLOCKS = 30
SIDE_ROWS = 8 * BLOCKS
QUARTER = 96
ROUTES = ((4, 1), (-4, 0), (1, 3), (-1, 2))
F32 = jnp.float32


def derivative_matrix():
    points = np.array([-1.0, -np.sqrt(3.0 / 7.0), 0.0, np.sqrt(3.0 / 7.0), 1.0])
    weights = [1.0 / np.prod([points[a] - points[b] for b in range(5) if b != a]) for a in range(5)]
    matrix = np.zeros((5, 5))
    for a in range(5):
        for b in range(5):
            if a != b:
                matrix[a, b] = weights[b] / weights[a] / (points[a] - points[b])
        matrix[a, a] = -np.sum(matrix[a])
    return matrix


D = derivative_matrix()


def line_derivative(u):
    e0, o0 = u[0] + u[4], u[0] - u[4]
    e1, o1 = u[1] + u[3], u[1] - u[3]
    even = [
        float((D[a, 0] + D[a, 4]) / 2) * e0 + float((D[a, 1] + D[a, 3]) / 2) * e1 + float(D[a, 2]) * u[2]
        for a in (0, 1)
    ]
    odd = [float((D[a, 0] - D[a, 4]) / 2) * o0 + float((D[a, 1] - D[a, 3]) / 2) * o1 for a in (0, 1, 2)]
    return [odd[0] + even[0], odd[1] + even[1], odd[2], odd[1] - even[1], odd[0] - even[0]]


def rows(field, node, count=1, nodes=125):
    start = 8 * (nodes * field + node)
    if not isinstance(start, int):
        start = pl.multiple_of(start, 8)
    return pl.ds(start, 8 * count)


def face_node(face, p, q):
    fixed = 0 if face % 2 == 0 else 4
    if face < 2:
        return 25 * fixed + 5 * p + q
    if face < 4:
        return 25 * p + 5 * fixed + q
    return 25 * p + 5 * q + fixed


def iotas():
    row = lax.broadcasted_iota(jnp.int32, (8, 128), 0)
    lane = lax.broadcasted_iota(jnp.int32, (8, 128), 1)
    return row, lane, row // 4


def pick(x, index):
    return jnp.take_along_axis(x, index, axis=1, mode="promise_in_bounds")


def other_half(x):
    return pltpu.roll(x, 4, 0)


def pack_sides(u, lists, s):
    row, lane, half = iotas()
    group = half * 4 + lane // 32
    sides = []
    for side in range(4):
        listed = jnp.tile(jnp.broadcast_to(lists[0, side : side + 1, :], (8, 32)), (1, 4))
        sides.append((listed & 127, (listed >> 7) == half, listed < 256))

    def body(p, carry):
        for side, (index, here, listed_slot) in enumerate(sides):
            packed = None
            for column in range(45):
                q, field = divmod(column, 9)
                x = u[rows(field, face_node(side, p, q)), :]
                value = pick(x, index)
                value = jnp.where(here, value, other_half(value))
                t = column % 8
                packed = value if t == 0 else jnp.where(group == t, value, packed)
                if t == 7 or column == 44:
                    s[rows(side * BLOCKS + p * 6 + column // 8, 0, nodes=1), :] = jnp.where(listed_slot, packed, 0.0)
        return carry

    lax.fori_loop(0, 5, body, 0)


def state_copies(packed, arrays, sems, inward):
    view = packed.reshape(1125, 8, 128)
    copies = []
    for kind, array in enumerate(arrays):
        for h in range(2):
            inside, outside = view.at[:, pl.ds(4 * h + 2 * kind, 2), :], array.at[:, h]
            pair = (outside, inside) if inward else (inside, outside)
            copies.append(pltpu.make_async_copy(*pair, sems.at[2 * kind + h]))
    return copies


X_FIELDS = (0, 1, 2, 3, 8, 7)
Y_FIELDS = (0, 1, 2, 8, 4, 6)
Z_FIELDS = (0, 1, 2, 7, 6, 5)


def volume(u, m, codes, a, gx, gy, gz, part, with_faces):
    x_faces = local_faces(codes, (0, 1), u) if with_faces else None

    def x_lines(j, carry):
        for slot, field in enumerate(X_FIELDS):
            lines = [u[rows(field, 25 * i + 5 * j, 5), :] for i in range(5)]
            for i, value in enumerate(line_derivative(lines)):
                gx[rows(slot, 25 * i + 5 * j, 5), :] = value
        if not with_faces:
            return carry
        for face in (0, 1):
            jumps, mirror = x_faces[face]
            for q in range(5):
                n = face_node(face, j, q)
                medium = [m[rows(c, n), :] for c in range(3)]
                own = [u[rows(field, n), :] for field in range(9)]
                amounts = corrections(face, jumps(j, q, own), medium, wave_speed(medium), mirror)
                for field in range(9):
                    a[rows(field, n), :] = own[field] + amounts[field]
        for i in (1, 2, 3):
            for field in range(9):
                place = rows(field, 25 * i + 5 * j, 5)
                a[place, :] = u[place, :]
        return carry

    lax.fori_loop(0, 5, x_lines, 0)
    other_faces = local_faces(codes, (2, 3, 4, 5), u) if with_faces else None

    def slab(i, carry):
        for slot, field in enumerate(Y_FIELDS):
            lines = [u[rows(field, 25 * i + 5 * j, 5), :] for j in range(5)]
            for j, value in enumerate(line_derivative(lines)):
                gy[rows(slot, 5 * j, 5, nodes=25), :] = value
        for slot, field in enumerate(Z_FIELDS):
            for j in range(5):
                lines = [u[rows(field, 25 * i + 5 * j + k), :] for k in range(5)]
                for k, value in enumerate(line_derivative(lines)):
                    gz[rows(slot, 5 * j + k, nodes=25), :] = value
        for j in range(5):
            for k in range(5):
                n = 25 * i + 5 * j + k
                x = [gx[rows(slot, n), :] for slot in range(6)]
                y = [gy[rows(slot, 5 * j + k, nodes=25), :] for slot in range(6)]
                z = [gz[rows(slot, 5 * j + k, nodes=25), :] for slot in range(6)]
                state = [u[rows(field, n), :] for field in range(9)]
                out = [a[rows(field, n), :] for field in range(9)] if with_faces else list(state)
                medium = lam, mu, buoy = [m[rows(c, n), :] for c in range(3)]
                divergence = x[0] + y[1] + z[2]
                sdiv = [x[3] + y[3] + z[3], x[4] + y[4] + z[4], x[5] + y[5] + z[5]]
                shear = [y[2] + z[1], x[2] + z[0], x[1] + y[0]]
                diagonal = [x[0], y[1], z[2]]
                pressure = lam * divergence
                twice = mu + mu
                for b in range(3):
                    out[b] = out[b] + buoy * sdiv[b]
                    out[3 + b] = out[3 + b] + (pressure + twice * diagonal[b])
                    out[6 + b] = out[6 + b] + mu * shear[b]
                touching = [(face, q) for face, at, q in ((2, j == 0, k), (3, j == 4, k), (4, k == 0, j), (5, k == 4, j)) if at]
                if with_faces and touching:
                    speed = wave_speed(medium)
                    for face, q in touching:
                        jumps, mirror = other_faces[face]
                        amounts = corrections(face, jumps(i, q, state), medium, speed, mirror)
                        out = [x + y for x, y in zip(out, amounts)]
                for field in range(9):
                    a[rows(field, n), :] = out[field]
                dual = [pltpu.roll(v, 6, 0) for v in state]
                part[rows(0, n), :] = divergence * (dual[3] + dual[4] + dual[5])
                normal = diagonal[0] * dual[3] + diagonal[1] * dual[4] + diagonal[2] * dual[5]
                tangent = shear[0] * dual[6] + shear[1] * dual[7] + shear[2] * dual[8]
                part[rows(1, n), :] = (normal + normal) + tangent
                part[rows(2, n), :] = sdiv[0] * dual[0] + sdiv[1] * dual[1] + sdiv[2] * dual[2]
        return carry

    lax.fori_loop(0, 5, slab, 0)


def sum_shots(part, total, earlier=None):
    for c in range(3):
        for block in range(16):
            size = 8 if block < 15 else 5
            for h in range(2):
                start = 1000 * c + 64 * block + 4 * h
                value = part[pl.ds(start, size, stride=8), :] + part[pl.ds(start + 1, size, stride=8), :]
                where = (pl.ds(128 * c + 8 * block, size), pl.ds(128 * h, 128))
                if earlier is not None:
                    value = value + earlier[where]
                if size < 8:
                    total[pl.ds(128 * c + 8 * block, 8), pl.ds(128 * h, 128)] = jnp.zeros((8, 128), F32)
                total[where] = value


def dom_peer(offset):
    d = lax.axis_index("dom")
    return lax.rem(d + offset + N_DOM, N_DOM)


def greet(shots):
    barrier = pltpu.get_barrier_semaphore()
    for offset, side in ROUTES:
        pl.semaphore_signal(barrier, inc=1, device_id={"dom": dom_peer(offset)}, device_id_type=MESH)
    if shots:
        me = lax.axis_index("shot")
        for step in range(1, N_SHOT):
            peer = lax.rem(me + step, N_SHOT)
            pl.semaphore_signal(barrier, inc=1, device_id={"shot": peer}, device_id_type=MESH)


def greeted(shots):
    pl.semaphore_wait(pltpu.get_barrier_semaphore(), 4 + (3 if shots else 0))


def start_sides(s, ghosts, send_sem, recv_sem):
    copies = []
    for b, (offset, side) in enumerate(ROUTES):
        copy = pltpu.make_async_remote_copy(
            src_ref=s.at[pl.ds(side * SIDE_ROWS, SIDE_ROWS)],
            dst_ref=ghosts.at[pl.ds(b * SIDE_ROWS, SIDE_ROWS)],
            send_sem=send_sem.at[b],
            recv_sem=recv_sem.at[b],
            device_id={"dom": dom_peer(offset)},
            device_id_type=MESH,
        )
        copy.start()
        copies.append(copy)
    return copies


def first_kernel(
    count, fw, ad, mat, lists, codes, u, m, a, ghosts, total, s, gx, gy, gz, part, jumps, send_sem, recv_sem, sems
):
    greet(False)
    row, lane, half = iotas()
    copies = state_copies(u, (fw, ad), sems, True)
    for copy in copies:
        copy.start()

    def per_kind(c, carry):
        for h in range(2):
            for block in range(16):
                size = 8 if block < 15 else 5
                x = 0.01 * mat[c, pl.ds(8 * block, size), pl.ds(128 * h, 128)]
                for ks in range(4):
                    m[pl.ds(c * 1000 + 64 * block + 4 * h + ks, size, stride=8), :] = x
        return carry

    lax.fori_loop(0, 3, per_kind, 0)
    for copy in copies:
        copy.wait()
    live = lane + 128 * half < count[0]

    def mask(group, carry):
        for n in range(25):
            place = rows(0, 25 * group + n)
            u[place, :] = jnp.where(live, u[place, :], 0.0)
        return carry

    lax.fori_loop(0, 45, mask, 0)
    pack_sides(u, lists, s)
    greeted(False)
    copies = start_sides(s, ghosts, send_sem, recv_sem)
    volume(u, m, codes, a, gx, gy, gz, part, True)
    sum_shots(part, total)
    for copy in copies:
        copy.wait()
    add_ghosts(m, ghosts, codes, a, jumps)


def second_kernel(
    u, m, codes, lists, earlier, a, ghosts, gradient, s, gx, gy, gz, part, jumps, mine, theirs,
    send_sem, recv_sem, reduce_send, reduce_recv, spread_send, spread_recv,
):
    greet(True)
    pack_sides(u, lists, s)
    greeted(True)
    copies = start_sides(s, ghosts, send_sem, recv_sem)
    volume(u, m, codes, a, gx, gy, gz, part, False)
    sum_shots(part, mine, earlier)
    me = lax.axis_index("shot")

    def piece(owner):
        return pl.ds(pl.multiple_of(QUARTER * owner, 8), QUARTER)

    def exchange(source, target, sends, receives, step):
        return pltpu.make_async_remote_copy(
            src_ref=source,
            dst_ref=target,
            send_sem=sends.at[step - 1],
            recv_sem=receives.at[step - 1],
            device_id={"shot": lax.rem(me + step, N_SHOT)},
            device_id_type=MESH,
        )

    outgoing = [
        exchange(mine.at[piece(lax.rem(me + step, N_SHOT))], theirs.at[step - 1], reduce_send, reduce_recv, step)
        for step in (2, 1, 3)
    ]
    for copy in outgoing:
        copy.start()
    add_local_faces((0, 1), u, m, codes, a)
    add_local_faces((2, 3), u, m, codes, a)
    for copy in outgoing:
        copy.wait_recv()
    own = piece(me)
    gradient[own, :] = 0.005 * (mine[own, :] + theirs[0] + theirs[1] + theirs[2])
    spread = [exchange(gradient.at[own], gradient.at[own], spread_send, spread_recv, step) for step in (2, 1, 3)]
    for copy in spread:
        copy.start()
    add_local_faces((4, 5), u, m, codes, a)
    for copy in copies:
        copy.wait()
    add_ghosts(m, ghosts, codes, a, jumps)
    for copy in outgoing:
        copy.wait_send()
    for copy in spread:
        copy.wait()


def corrections(face, jump, medium, speed, mirror=None, weight=1.0):
    axis = face // 2
    sign = -1.0 if face % 2 == 0 else 1.0
    lam, mu, buoy = medium
    speed_v = speed_s = speed if weight == 1.0 else weight * speed
    kb, kl, km = ((5.0 * weight * sign) * x for x in (buoy, lam, mu))
    if mirror is not None:
        speed_v, kl, km = (x * mirror[0] for x in (speed_v, kl, km))
        speed_s, kb = (x * mirror[1] for x in (speed_s, kb))
    out = [kb * jump[SLOTS[b][axis]] + speed_v * jump[b] for b in range(3)]
    pressure = kl * jump[axis]
    for pair, (b, c) in enumerate(PAIRS):
        amount = speed_s * jump[3 + pair]
        if b == c:
            amount = amount + pressure
        if axis == b and axis == c:
            amount = amount + (km + km) * jump[axis]
        elif axis == b:
            amount = amount + km * jump[c]
        elif axis == c:
            amount = amount + km * jump[b]
        out.append(amount)
    return out


def wave_speed(medium):
    lam, mu, buoy = medium
    return 5.0 * jnp.sqrt((lam + 2.0 * mu) * buoy)


def add_face(face, p, m, target, jump_of, weight=1.0):
    for q in range(5):
        n = face_node(face, p, q)
        medium = [m[rows(c, n), :] for c in range(3)]
        jump = [jump_of(q, field) for field in range(9)]
        for field, amount in enumerate(corrections(face, jump, medium, wave_speed(medium), weight=weight)):
            place = rows(field, n)
            target[place, :] = target[place, :] + amount


def face_code(codes, face, half):
    low = jnp.broadcast_to(codes[0:1, 256 * face : 256 * face + 128], (8, 128))
    high = jnp.broadcast_to(codes[0:1, 256 * face + 128 : 256 * face + 256], (8, 128))
    return jnp.where(half == 0, low, high)


def local_faces(codes, faces, u):
    row, lane, half = iotas()
    found = {}
    for face in faces:
        code = face_code(codes, face, half)
        local = (code >> 8) == (face ^ 1)
        index = code & 127
        same = ((code >> 7) & 1) == half
        free = code == 1664
        mirror = jnp.where(free, 0.0, 1.0), jnp.where(free, 2.0, 1.0)

        def jumps(p, q, own, face=face, local=local, index=index, same=same):
            out = []
            for field in range(9):
                x = u[rows(field, face_node(face ^ 1, p, q)), :]
                value = jnp.where(same, pick(x, index), pick(other_half(x), index))
                out.append(jnp.where(local, value, 0.0) - own[field])
            return out

        found[face] = (jumps, mirror)
    return found


def add_local_faces(faces, u, m, codes, target):
    found = local_faces(codes, faces, u)

    def body(p, carry):
        for face in faces:
            jumps, mirror = found[face]
            for q in range(5):
                n = face_node(face, p, q)
                medium = [m[rows(c, n), :] for c in range(3)]
                own = [u[rows(field, n), :] for field in range(9)]
                amounts = corrections(face, jumps(p, q, own), medium, wave_speed(medium), mirror)
                for field, amount in enumerate(amounts):
                    place = rows(field, n)
                    target[place, :] = target[place, :] + amount
        return carry

    lax.fori_loop(0, 5, body, 0)


def presence():
    d = lax.axis_index("dom")
    return [jnp.where((d - offset >= 0) & (d - offset < N_DOM), 1, 0) for offset, side in ROUTES]


def ghost_mask(code, b, present):
    return ((code >> 5) == 48 + b) & (jnp.broadcast_to(present[b], (8, 128)) == 1)


def add_ghosts(m, ghosts, codes, target, scratch):
    row, lane, half = iotas()
    present = presence()
    sides = []
    for face in range(4):
        code = face_code(codes, face, half)
        sides.append((ghost_mask(code, face, present), [(code & 31) + 32 * c for c in range(4)]))

    def body(p, carry):
        for face, (ghost, index) in enumerate(sides):
            blocks = []
            for block in range(6):
                g = ghosts[rows(face * BLOCKS + 6 * p + block, 0, nodes=1), :]
                swapped = other_half(g)
                blocks.append((jnp.where(half == 0, g, swapped), jnp.where(half == 1, g, swapped)))
            for c in range(4):
                for column in range(45):
                    block, t = divmod(column, 8)
                    if t % 4 == c:
                        value = jnp.where(ghost, pick(blocks[block][t // 4], index[c]), 0.0)
                        scratch[rows(45 * face + column, 0, nodes=1), :] = value
        for face in range(4):
            add_face(face, p, m, target, lambda q, field: scratch[rows(45 * face + 9 * q + field, 0, nodes=1), :])
        return carry

    lax.fori_loop(0, 5, body, 0)


def other_exteriors(u, m, ghosts, codes, target, scratch, weight=1.0):
    row, lane, half = iotas()
    present = presence()
    face_codes, odd = [], jnp.zeros((8, 128), F32)
    for face in range(6):
        code = face_code(codes, face, half)
        face_codes.append(code)
        usual = ((code >> 8) == (face ^ 1)) | (code >= 1664)
        if face < 4:
            usual = usual | ((code >> 5) == 48 + face)
        odd = odd + jnp.where(usual, 0.0, 1.0)

    @pl.when(jnp.sum(odd) > 0.0)
    def _():
        for face in range(6):
            code = face_codes[face]
            index = code & 127
            same = ((code >> 7) & 1) == half

            def body(p, carry, face=face, code=code, index=index, same=same):
                def column_body(column, inner):
                    q = column // 9
                    field = column - 9 * q
                    value = jnp.zeros((8, 128), F32)
                    for g in range(6):
                        if g != face ^ 1:
                            x = u[rows(field, face_node(g, p, q)), :]
                            found = jnp.where(same, pick(x, index), pick(other_half(x), index))
                            value = jnp.where((code >> 8) == g, found, value)
                    block = column // 8
                    t = column - 8 * block
                    upper = t // 4
                    for b in range(4):
                        if b != face:
                            x = ghosts[rows(b * BLOCKS + 6 * p + block, 0, nodes=1), :]
                            x = jnp.where(half == upper, x, other_half(x))
                            found = pick(x, (code & 31) + 32 * (t - 4 * upper))
                            value = jnp.where(ghost_mask(code, b, present), found, value)
                    scratch[rows(column, 0, nodes=1), :] = value
                    return inner

                lax.fori_loop(0, 45, column_body, 0)

                def jump_of(q, field):
                    return scratch[rows(9 * q + field, 0, nodes=1), :]

                add_face(face, p, m, target, jump_of, weight=weight)
                return carry

            lax.fori_loop(0, 5, body, 0)


def middle_kernel(u, m, ghosts, codes, a, target, scratch):
    other_exteriors(u, m, ghosts, codes, target, scratch)


def last_kernel(u, m, ghosts, codes, a, start, reduced, fw, ad, gradient, end, scratch, sems):
    def average(group, carry):
        for n in range(25):
            place = rows(0, 25 * group + n)
            end[place, :] = 0.5 * start[place, :] + 0.5 * a[place, :]
        return carry

    lax.fori_loop(0, 45, average, 0)
    other_exteriors(u, m, ghosts, codes, end, scratch, 0.5)
    copies = state_copies(end, (fw, ad), sems, False)
    for copy in copies:
        copy.start()
    for c in range(3):
        gradient[c, :, :] = reduced[pl.ds(128 * c, 125), :]
    for copy in copies:
        copy.wait()


def vmem(count):
    return [pl.BlockSpec(memory_space=pltpu.VMEM)] * count


def shape(*dims):
    return jax.ShapeDtypeStruct(dims, F32)


def kept(*dims):
    return pltpu.VMEM(dims, F32)


def outer(*arrays):
    return [pltpu.with_memory_space_constraint(x, pltpu.HBM) for x in arrays]


def keep(*arrays):
    return [pltpu.with_memory_space_constraint(x, pltpu.VMEM) for x in arrays]


STATE = kept(9000, 128)
SIDES = kept(4 * SIDE_ROWS, 128)
TOTALS = kept(384, 256)
VOLUME_SCRATCH = [SIDES, kept(6000, 128), kept(1200, 128), kept(1200, 128), kept(3000, 128), kept(1440, 128)]
HBM = pl.BlockSpec(memory_space=pltpu.HBM)
GRANT = 20 << 20


def copies_semaphore(count):
    return pltpu.SemaphoreType.DMA((count,))


def first_call(counts, forward, adjoint, material, lists, codes):
    return pl.pallas_call(
        first_kernel,
        out_shape=(STATE, kept(3000, 128), STATE, SIDES, TOTALS),
        in_specs=[pl.BlockSpec(memory_space=pltpu.SMEM), HBM, HBM] + vmem(3),
        out_specs=tuple(vmem(5)),
        scratch_shapes=VOLUME_SCRATCH + [copies_semaphore(4)] * 3,
        compiler_params=pltpu.CompilerParams(collective_id=0, has_side_effects=True, vmem_limit_bytes=GRANT),
        name="first",
    )(counts, *outer(forward, adjoint), material, lists, codes)


def second_call(u, m, codes, lists, earlier):
    return pl.pallas_call(
        second_kernel,
        out_shape=(STATE, SIDES, TOTALS),
        in_specs=vmem(5),
        out_specs=tuple(vmem(3)),
        scratch_shapes=VOLUME_SCRATCH
        + [TOTALS, kept(3, QUARTER, 256)]
        + [copies_semaphore(4)] * 2
        + [copies_semaphore(3)] * 4,
        compiler_params=pltpu.CompilerParams(collective_id=1, has_side_effects=True, vmem_limit_bytes=GRANT),
        name="second",
    )(*keep(u, m), codes, lists, *keep(earlier))


def middle_call(u, m, ghosts, codes, a):
    return pl.pallas_call(
        middle_kernel,
        out_shape=STATE,
        in_specs=vmem(5),
        out_specs=vmem(1)[0],
        scratch_shapes=[pltpu.VMEM((360, 128), F32)],
        input_output_aliases={4: 0},
        compiler_params=pltpu.CompilerParams(vmem_limit_bytes=GRANT),
        name="middle",
    )(*keep(u, m, ghosts), codes, *keep(a))


def last_call(u, m, ghosts, codes, a, start, reduced):
    return pl.pallas_call(
        last_kernel,
        out_shape=(shape(1125, 2, 2, 128), shape(1125, 2, 2, 128), shape(3, 125, 256)),
        in_specs=vmem(7),
        out_specs=(HBM, HBM, vmem(1)[0]),
        scratch_shapes=[
            pltpu.VMEM((9000, 128), F32),
            pltpu.VMEM((360, 128), F32),
            pltpu.SemaphoreType.DMA((4,)),
        ],
        compiler_params=pltpu.CompilerParams(vmem_limit_bytes=GRANT),
        name="last",
    )(*keep(u, m, ghosts), codes, *keep(a, start, reduced))


def as_rows(x):
    return x.reshape(2, 9, 125, 2, 128).transpose(1, 2, 3, 0, 4).reshape(1125, 2, 2, 128)


def as_array(x):
    return x.reshape(9, 125, 2, 2, 128).transpose(3, 0, 1, 2, 4).reshape(2, 9, 125, 256)


def shards(forward, adjoint, material, counts, send_list, neighbours):
    u0, m, a1, ghosts, earlier = first_call(
        counts, as_rows(forward), as_rows(adjoint), material, send_list, neighbours
    )
    u1 = middle_call(u0, m, ghosts, neighbours, a1)
    a2, ghosts2, reduced = second_call(u1, m, neighbours, send_list, earlier)
    fw, ad, gradient = last_call(u1, m, ghosts2, neighbours, a2, u0, reduced)
    return as_array(fw), as_array(ad), gradient


def solution(mesh):
    placed = (
        P("shot", None, None, "dom"),
        P("shot", None, None, "dom"),
        P(None, None, "dom"),
        P("dom"),
        P("dom", None, None),
        P("dom", None),
    )
    return jax.shard_map(
        shards,
        mesh=mesh,
        in_specs=placed,
        out_specs=placed[:3],
        check_vma=False,
    )
```

```python
import functools

import jax
import jax.numpy as jnp
import numpy as np
from jax import lax
from jax.experimental import pallas as pl
from jax.experimental.pallas import tpu as pltpu
from jax.sharding import PartitionSpec as P

MESH = pl.DeviceIdType.MESH
PAIRS = ((0, 0), (1, 1), (2, 2), (1, 2), (0, 2), (0, 1))
SLOTS = ((3, 8, 7), (8, 4, 6), (7, 6, 5))
N_DOM = 64
N_SHOT = 4
BLOCKS = 30
SIDE_ROWS = 8 * BLOCKS
QUARTER = 96
ROUTES = ((4, 1), (-4, 0), (1, 3), (-1, 2))
F32 = jnp.float32


def derivative_matrix():
    points = np.array([-1.0, -np.sqrt(3.0 / 7.0), 0.0, np.sqrt(3.0 / 7.0), 1.0])
    weights = [1.0 / np.prod([points[a] - points[b] for b in range(5) if b != a]) for a in range(5)]
    matrix = np.zeros((5, 5))
    for a in range(5):
        for b in range(5):
            if a != b:
                matrix[a, b] = weights[b] / weights[a] / (points[a] - points[b])
        matrix[a, a] = -np.sum(matrix[a])
    return matrix


D = derivative_matrix()


def line_derivative(u):
    e0, o0 = u[0] + u[4], u[0] - u[4]
    e1, o1 = u[1] + u[3], u[1] - u[3]
    even = [
        float((D[a, 0] + D[a, 4]) / 2) * e0 + float((D[a, 1] + D[a, 3]) / 2) * e1 + float(D[a, 2]) * u[2]
        for a in (0, 1)
    ]
    odd = [float((D[a, 0] - D[a, 4]) / 2) * o0 + float((D[a, 1] - D[a, 3]) / 2) * o1 for a in (0, 1, 2)]
    return [odd[0] + even[0], odd[1] + even[1], odd[2], odd[1] - even[1], odd[0] - even[0]]


def rows(field, node, count=1, nodes=125):
    start = 8 * (nodes * field + node)
    if not isinstance(start, int):
        start = pl.multiple_of(start, 8)
    return pl.ds(start, 8 * count)


def face_node(face, p, q):
    fixed = 0 if face % 2 == 0 else 4
    if face < 2:
        return 25 * fixed + 5 * p + q
    if face < 4:
        return 25 * p + 5 * fixed + q
    return 25 * p + 5 * q + fixed


def iotas():
    row = lax.broadcasted_iota(jnp.int32, (8, 128), 0)
    lane = lax.broadcasted_iota(jnp.int32, (8, 128), 1)
    return row, lane, row // 4


def pick(x, index):
    return jnp.take_along_axis(x, index, axis=1, mode="promise_in_bounds")


def other_half(x):
    return pltpu.roll(x, 4, 0)


def pack_sides(u, lists, s):
    row, lane, half = iotas()
    group = half * 4 + lane // 32
    sides = []
    for side in range(4):
        listed = jnp.tile(jnp.broadcast_to(lists[0, side : side + 1, :], (8, 32)), (1, 4))
        sides.append((listed & 127, (listed >> 7) == half, listed < 256))

    def body(p, carry):
        for side, (index, here, listed_slot) in enumerate(sides):
            packed = None
            for column in range(45):
                q, field = divmod(column, 9)
                x = u[rows(field, face_node(side, p, q)), :]
                value = pick(x, index)
                value = jnp.where(here, value, other_half(value))
                t = column % 8
                packed = value if t == 0 else jnp.where(group == t, value, packed)
                if t == 7 or column == 44:
                    s[rows(side * BLOCKS + p * 6 + column // 8, 0, nodes=1), :] = jnp.where(listed_slot, packed, 0.0)
        return carry

    lax.fori_loop(0, 5, body, 0)


def state_copies(packed, arrays, sems, inward):
    view = packed.reshape(1125, 8, 128)
    copies = []
    for kind, array in enumerate(arrays):
        for h in range(2):
            inside, outside = view.at[:, pl.ds(4 * h + 2 * kind, 2), :], array.at[:, h]
            pair = (outside, inside) if inward else (inside, outside)
            copies.append(pltpu.make_async_copy(*pair, sems.at[2 * kind + h]))
    return copies


X_FIELDS = (0, 1, 2, 3, 8, 7)
Y_FIELDS = (0, 1, 2, 8, 4, 6)
Z_FIELDS = (0, 1, 2, 7, 6, 5)


def volume(u, m, codes, a, gx, gy, gz, part, with_faces):
    x_faces = local_faces(codes, (0, 1), u) if with_faces else None

    def x_lines(j, carry):
        for slot, field in enumerate(X_FIELDS):
            lines = [u[rows(field, 25 * i + 5 * j, 5), :] for i in range(5)]
            for i, value in enumerate(line_derivative(lines)):
                gx[rows(slot, 25 * i + 5 * j, 5), :] = value
        if not with_faces:
            return carry
        for face in (0, 1):
            jumps, mirror = x_faces[face]
            for q in range(5):
                n = face_node(face, j, q)
                medium = [m[rows(c, n), :] for c in range(3)]
                own = [u[rows(field, n), :] for field in range(9)]
                amounts = corrections(face, jumps(j, q, own), medium, wave_speed(medium), mirror)
                for field in range(9):
                    a[rows(field, n), :] = own[field] + amounts[field]
        for i in (1, 2, 3):
            for field in range(9):
                place = rows(field, 25 * i + 5 * j, 5)
                a[place, :] = u[place, :]
        return carry

    lax.fori_loop(0, 5, x_lines, 0)
    other_faces = local_faces(codes, (2, 3, 4, 5), u) if with_faces else None

    def slab(i, carry):
        for slot, field in enumerate(Y_FIELDS):
            lines = [u[rows(field, 25 * i + 5 * j, 5), :] for j in range(5)]
            for j, value in enumerate(line_derivative(lines)):
                gy[rows(slot, 5 * j, 5, nodes=25), :] = value
        for slot, field in enumerate(Z_FIELDS):
            for j in range(5):
                lines = [u[rows(field, 25 * i + 5 * j + k), :] for k in range(5)]
                for k, value in enumerate(line_derivative(lines)):
                    gz[rows(slot, 5 * j + k, nodes=25), :] = value
        for j in range(5):
            for k in range(5):
                n = 25 * i + 5 * j + k
                x = [gx[rows(slot, n), :] for slot in range(6)]
                y = [gy[rows(slot, 5 * j + k, nodes=25), :] for slot in range(6)]
                z = [gz[rows(slot, 5 * j + k, nodes=25), :] for slot in range(6)]
                state = [u[rows(field, n), :] for field in range(9)]
                out = [a[rows(field, n), :] for field in range(9)] if with_faces else list(state)
                medium = lam, mu, buoy = [m[rows(c, n), :] for c in range(3)]
                divergence = x[0] + y[1] + z[2]
                sdiv = [x[3] + y[3] + z[3], x[4] + y[4] + z[4], x[5] + y[5] + z[5]]
                shear = [y[2] + z[1], x[2] + z[0], x[1] + y[0]]
                diagonal = [x[0], y[1], z[2]]
                pressure = lam * divergence
                twice = mu + mu
                for b in range(3):
                    out[b] = out[b] + buoy * sdiv[b]
                    out[3 + b] = out[3 + b] + (pressure + twice * diagonal[b])
                    out[6 + b] = out[6 + b] + mu * shear[b]
                touching = [(face, q) for face, at, q in ((2, j == 0, k), (3, j == 4, k), (4, k == 0, j), (5, k == 4, j)) if at]
                if with_faces and touching:
                    speed = wave_speed(medium)
                    for face, q in touching:
                        jumps, mirror = other_faces[face]
                        amounts = corrections(face, jumps(i, q, state), medium, speed, mirror)
                        out = [x + y for x, y in zip(out, amounts)]
                for field in range(9):
                    a[rows(field, n), :] = out[field]
                dual = [pltpu.roll(v, 6, 0) for v in state]
                part[rows(0, n), :] = divergence * (dual[3] + dual[4] + dual[5])
                normal = diagonal[0] * dual[3] + diagonal[1] * dual[4] + diagonal[2] * dual[5]
                tangent = shear[0] * dual[6] + shear[1] * dual[7] + shear[2] * dual[8]
                part[rows(1, n), :] = (normal + normal) + tangent
                part[rows(2, n), :] = sdiv[0] * dual[0] + sdiv[1] * dual[1] + sdiv[2] * dual[2]
        return carry

    lax.fori_loop(0, 5, slab, 0)


def sum_shots(part, total, earlier=None):
    for c in range(3):
        for block in range(16):
            size = 8 if block < 15 else 5
            for h in range(2):
                start = 1000 * c + 64 * block + 4 * h
                value = part[pl.ds(start, size, stride=8), :] + part[pl.ds(start + 1, size, stride=8), :]
                where = (pl.ds(128 * c + 8 * block, size), pl.ds(128 * h, 128))
                if earlier is not None:
                    value = value + earlier[where]
                if size < 8:
                    total[pl.ds(128 * c + 8 * block, 8), pl.ds(128 * h, 128)] = jnp.zeros((8, 128), F32)
                total[where] = value


def dom_peer(offset):
    d = lax.axis_index("dom")
    return lax.rem(d + offset + N_DOM, N_DOM)


def greet(shots):
    barrier = pltpu.get_barrier_semaphore()
    for offset, side in ROUTES:
        pl.semaphore_signal(barrier, inc=1, device_id={"dom": dom_peer(offset)}, device_id_type=MESH)
    if shots:
        me = lax.axis_index("shot")
        for step in range(1, N_SHOT):
            peer = lax.rem(me + step, N_SHOT)
            pl.semaphore_signal(barrier, inc=1, device_id={"shot": peer}, device_id_type=MESH)


def greeted(shots):
    pl.semaphore_wait(pltpu.get_barrier_semaphore(), 4 + (3 if shots else 0))


def start_sides(s, ghosts, send_sem, recv_sem):
    copies = []
    for b, (offset, side) in enumerate(ROUTES):
        copy = pltpu.make_async_remote_copy(
            src_ref=s.at[pl.ds(side * SIDE_ROWS, SIDE_ROWS)],
            dst_ref=ghosts.at[pl.ds(b * SIDE_ROWS, SIDE_ROWS)],
            send_sem=send_sem.at[b],
            recv_sem=recv_sem.at[b],
            device_id={"dom": dom_peer(offset)},
            device_id_type=MESH,
        )
        copy.start()
        copies.append(copy)
    return copies


def first_kernel(
    count, fw, ad, mat_in, lists_in, codes_in, u, m, a, ghosts, total, lists, codes,
    s, gx, gy, gz, part, jumps, send_sem, recv_sem, sems, mat, small_sems
):
    greet(False)
    row, lane, half = iotas()
    small = [
        pltpu.make_async_copy(source, target, small_sems.at[k])
        for k, (source, target) in enumerate(((mat_in, mat), (lists_in, lists), (codes_in, codes)))
    ]
    copies = state_copies(u, (fw, ad), sems, True)
    for copy in small + copies:
        copy.start()
    small[0].wait()

    def per_kind(c, carry):
        for h in range(2):
            for block in range(16):
                size = 8 if block < 15 else 5
                x = 0.01 * mat[c, pl.ds(8 * block, size), pl.ds(128 * h, 128)]
                for ks in range(4):
                    m[pl.ds(c * 1000 + 64 * block + 4 * h + ks, size, stride=8), :] = x
        return carry

    lax.fori_loop(0, 3, per_kind, 0)
    for copy in copies + small[1:]:
        copy.wait()
    live = lane + 128 * half < count[0]

    def mask(group, carry):
        for n in range(25):
            place = rows(0, 25 * group + n)
            u[place, :] = jnp.where(live, u[place, :], 0.0)
        return carry

    lax.fori_loop(0, 45, mask, 0)
    pack_sides(u, lists, s)
    greeted(False)
    copies = start_sides(s, ghosts, send_sem, recv_sem)
    volume(u, m, codes, a, gx, gy, gz, part, True)
    sum_shots(part, total)
    for copy in copies:
        copy.wait()
    add_ghosts(m, ghosts, codes, a, jumps)


def second_kernel(
    u, m, codes, lists, earlier, a, ghosts, gradient, s, gx, gy, gz, part, jumps, mine, theirs,
    send_sem, recv_sem, reduce_send, reduce_recv, spread_send, spread_recv,
):
    greet(True)
    pack_sides(u, lists, s)
    greeted(True)
    copies = start_sides(s, ghosts, send_sem, recv_sem)
    volume(u, m, codes, a, gx, gy, gz, part, False)
    sum_shots(part, mine, earlier)
    me = lax.axis_index("shot")

    def piece(owner):
        return pl.ds(pl.multiple_of(QUARTER * owner, 8), QUARTER)

    def exchange(source, target, sends, receives, step):
        return pltpu.make_async_remote_copy(
            src_ref=source,
            dst_ref=target,
            send_sem=sends.at[step - 1],
            recv_sem=receives.at[step - 1],
            device_id={"shot": lax.rem(me + step, N_SHOT)},
            device_id_type=MESH,
        )

    outgoing = [
        exchange(mine.at[piece(lax.rem(me + step, N_SHOT))], theirs.at[step - 1], reduce_send, reduce_recv, step)
        for step in (2, 1, 3)
    ]
    for copy in outgoing:
        copy.start()
    add_local_faces((0, 1), u, m, codes, a)
    add_local_faces((2, 3), u, m, codes, a)
    for copy in outgoing:
        copy.wait_recv()
    own = piece(me)
    gradient[own, :] = 0.005 * (mine[own, :] + theirs[0] + theirs[1] + theirs[2])
    spread = [exchange(gradient.at[own], gradient.at[own], spread_send, spread_recv, step) for step in (2, 1, 3)]
    for copy in spread:
        copy.start()
    add_local_faces((4, 5), u, m, codes, a)
    for copy in copies:
        copy.wait()
    add_ghosts(m, ghosts, codes, a, jumps)
    for copy in outgoing:
        copy.wait_send()
    for copy in spread:
        copy.wait()


def corrections(face, jump, medium, speed, mirror=None, weight=1.0):
    axis = face // 2
    sign = -1.0 if face % 2 == 0 else 1.0
    lam, mu, buoy = medium
    speed_v = speed_s = speed if weight == 1.0 else weight * speed
    kb, kl, km = ((5.0 * weight * sign) * x for x in (buoy, lam, mu))
    if mirror is not None:
        speed_v, kl, km = (x * mirror[0] for x in (speed_v, kl, km))
        speed_s, kb = (x * mirror[1] for x in (speed_s, kb))
    out = [kb * jump[SLOTS[b][axis]] + speed_v * jump[b] for b in range(3)]
    pressure = kl * jump[axis]
    for pair, (b, c) in enumerate(PAIRS):
        amount = speed_s * jump[3 + pair]
        if b == c:
            amount = amount + pressure
        if axis == b and axis == c:
            amount = amount + (km + km) * jump[axis]
        elif axis == b:
            amount = amount + km * jump[c]
        elif axis == c:
            amount = amount + km * jump[b]
        out.append(amount)
    return out


def wave_speed(medium):
    lam, mu, buoy = medium
    return 5.0 * jnp.sqrt((lam + 2.0 * mu) * buoy)


def add_face(face, p, m, target, jump_of, weight=1.0):
    for q in range(5):
        n = face_node(face, p, q)
        medium = [m[rows(c, n), :] for c in range(3)]
        jump = [jump_of(q, field) for field in range(9)]
        for field, amount in enumerate(corrections(face, jump, medium, wave_speed(medium), weight=weight)):
            place = rows(field, n)
            target[place, :] = target[place, :] + amount


def face_code(codes, face, half):
    low = jnp.broadcast_to(codes[0:1, 256 * face : 256 * face + 128], (8, 128))
    high = jnp.broadcast_to(codes[0:1, 256 * face + 128 : 256 * face + 256], (8, 128))
    return jnp.where(half == 0, low, high)


def local_faces(codes, faces, u):
    row, lane, half = iotas()
    found = {}
    for face in faces:
        code = face_code(codes, face, half)
        local = (code >> 8) == (face ^ 1)
        index = code & 127
        same = ((code >> 7) & 1) == half
        free = code == 1664
        mirror = jnp.where(free, 0.0, 1.0), jnp.where(free, 2.0, 1.0)

        def jumps(p, q, own, face=face, local=local, index=index, same=same):
            out = []
            for field in range(9):
                x = u[rows(field, face_node(face ^ 1, p, q)), :]
                value = jnp.where(same, pick(x, index), pick(other_half(x), index))
                out.append(jnp.where(local, value, 0.0) - own[field])
            return out

        found[face] = (jumps, mirror)
    return found


def add_local_faces(faces, u, m, codes, target):
    found = local_faces(codes, faces, u)

    def body(p, carry):
        for face in faces:
            jumps, mirror = found[face]
            for q in range(5):
                n = face_node(face, p, q)
                medium = [m[rows(c, n), :] for c in range(3)]
                own = [u[rows(field, n), :] for field in range(9)]
                amounts = corrections(face, jumps(p, q, own), medium, wave_speed(medium), mirror)
                for field, amount in enumerate(amounts):
                    place = rows(field, n)
                    target[place, :] = target[place, :] + amount
        return carry

    lax.fori_loop(0, 5, body, 0)


def presence():
    d = lax.axis_index("dom")
    return [jnp.where((d - offset >= 0) & (d - offset < N_DOM), 1, 0) for offset, side in ROUTES]


def ghost_mask(code, b, present):
    return ((code >> 5) == 48 + b) & (jnp.broadcast_to(present[b], (8, 128)) == 1)


def add_ghosts(m, ghosts, codes, target, scratch):
    row, lane, half = iotas()
    present = presence()
    sides = []
    for face in range(4):
        code = face_code(codes, face, half)
        sides.append((ghost_mask(code, face, present), [(code & 31) + 32 * c for c in range(4)]))

    def body(p, carry):
        for face, (ghost, index) in enumerate(sides):
            blocks = []
            for block in range(6):
                g = ghosts[rows(face * BLOCKS + 6 * p + block, 0, nodes=1), :]
                swapped = other_half(g)
                blocks.append((jnp.where(half == 0, g, swapped), jnp.where(half == 1, g, swapped)))
            for c in range(4):
                for column in range(45):
                    block, t = divmod(column, 8)
                    if t % 4 == c:
                        value = jnp.where(ghost, pick(blocks[block][t // 4], index[c]), 0.0)
                        scratch[rows(45 * face + column, 0, nodes=1), :] = value
        for face in range(4):
            add_face(face, p, m, target, lambda q, field: scratch[rows(45 * face + 9 * q + field, 0, nodes=1), :])
        return carry

    lax.fori_loop(0, 5, body, 0)


def other_exteriors(u, m, ghosts, codes, target, scratch, weight=1.0):
    row, lane, half = iotas()
    present = presence()
    face_codes, odd = [], jnp.zeros((8, 128), F32)
    for face in range(6):
        code = face_code(codes, face, half)
        face_codes.append(code)
        usual = ((code >> 8) == (face ^ 1)) | (code >= 1664)
        if face < 4:
            usual = usual | ((code >> 5) == 48 + face)
        odd = odd + jnp.where(usual, 0.0, 1.0)

    @pl.when(jnp.sum(odd) > 0.0)
    def _():
        for face in range(6):
            code = face_codes[face]
            index = code & 127
            same = ((code >> 7) & 1) == half

            def body(p, carry, face=face, code=code, index=index, same=same):
                def column_body(column, inner):
                    q = column // 9
                    field = column - 9 * q
                    value = jnp.zeros((8, 128), F32)
                    for g in range(6):
                        if g != face ^ 1:
                            x = u[rows(field, face_node(g, p, q)), :]
                            found = jnp.where(same, pick(x, index), pick(other_half(x), index))
                            value = jnp.where((code >> 8) == g, found, value)
                    block = column // 8
                    t = column - 8 * block
                    upper = t // 4
                    for b in range(4):
                        if b != face:
                            x = ghosts[rows(b * BLOCKS + 6 * p + block, 0, nodes=1), :]
                            x = jnp.where(half == upper, x, other_half(x))
                            found = pick(x, (code & 31) + 32 * (t - 4 * upper))
                            value = jnp.where(ghost_mask(code, b, present), found, value)
                    scratch[rows(column, 0, nodes=1), :] = value
                    return inner

                lax.fori_loop(0, 45, column_body, 0)

                def jump_of(q, field):
                    return scratch[rows(9 * q + field, 0, nodes=1), :]

                add_face(face, p, m, target, jump_of, weight=weight)
                return carry

            lax.fori_loop(0, 5, body, 0)


def middle_kernel(u, m, ghosts, codes, a, target, scratch):
    other_exteriors(u, m, ghosts, codes, target, scratch)


def last_kernel(u, m, ghosts, codes, a, start, reduced, fw, ad, gradient, end, scratch, sems):
    def average(group, carry):
        for n in range(25):
            place = rows(0, 25 * group + n)
            end[place, :] = 0.5 * start[place, :] + 0.5 * a[place, :]
        return carry

    lax.fori_loop(0, 45, average, 0)
    other_exteriors(u, m, ghosts, codes, end, scratch, 0.5)
    copies = state_copies(end, (fw, ad), sems, False)
    for copy in copies:
        copy.start()
    for c in range(3):
        gradient[c, :, :] = reduced[pl.ds(128 * c, 125), :]
    for copy in copies:
        copy.wait()


def vmem(count):
    return [pl.BlockSpec(memory_space=pltpu.VMEM)] * count


def shape(*dims):
    return jax.ShapeDtypeStruct(dims, F32)


def kept(*dims):
    return pltpu.VMEM(dims, F32)


def outer(*arrays):
    return [pltpu.with_memory_space_constraint(x, pltpu.HBM) for x in arrays]


def keep(*arrays):
    return [pltpu.with_memory_space_constraint(x, pltpu.VMEM) for x in arrays]


STATE = kept(9000, 128)
SIDES = kept(4 * SIDE_ROWS, 128)
TOTALS = kept(384, 256)
VOLUME_SCRATCH = [SIDES, kept(6000, 128), kept(1200, 128), kept(1200, 128), kept(3000, 128), kept(1440, 128)]
HBM = pl.BlockSpec(memory_space=pltpu.HBM)
GRANT = 20 << 20


def copies_semaphore(count):
    return pltpu.SemaphoreType.DMA((count,))


def first_call(counts, forward, adjoint, material, lists, codes):
    return pl.pallas_call(
        first_kernel,
        out_shape=(
            STATE, kept(3000, 128), STATE, SIDES, TOTALS,
            pltpu.VMEM(lists.shape, jnp.int32), pltpu.VMEM(codes.shape, jnp.int32),
        ),
        in_specs=[pl.BlockSpec(memory_space=pltpu.SMEM)] + [HBM] * 5,
        out_specs=tuple(vmem(7)),
        scratch_shapes=VOLUME_SCRATCH + [copies_semaphore(4)] * 3 + [kept(3, 125, 256), copies_semaphore(3)],
        compiler_params=pltpu.CompilerParams(collective_id=0, has_side_effects=True, vmem_limit_bytes=GRANT),
        name="first",
    )(counts, *outer(forward, adjoint, material, lists, codes))


def second_call(u, m, codes, lists, earlier):
    return pl.pallas_call(
        second_kernel,
        out_shape=(STATE, SIDES, TOTALS),
        in_specs=vmem(5),
        out_specs=tuple(vmem(3)),
        scratch_shapes=VOLUME_SCRATCH
        + [TOTALS, kept(3, QUARTER, 256)]
        + [copies_semaphore(4)] * 2
        + [copies_semaphore(3)] * 4,
        compiler_params=pltpu.CompilerParams(collective_id=1, has_side_effects=True, vmem_limit_bytes=GRANT),
        name="second",
    )(*keep(u, m, codes, lists, earlier))


def middle_call(u, m, ghosts, codes, a):
    return pl.pallas_call(
        middle_kernel,
        out_shape=STATE,
        in_specs=vmem(5),
        out_specs=vmem(1)[0],
        scratch_shapes=[pltpu.VMEM((360, 128), F32)],
        input_output_aliases={4: 0},
        compiler_params=pltpu.CompilerParams(vmem_limit_bytes=GRANT),
        name="middle",
    )(*keep(u, m, ghosts, codes, a))


def last_call(u, m, ghosts, codes, a, start, reduced):
    return pl.pallas_call(
        last_kernel,
        out_shape=(shape(1125, 2, 2, 128), shape(1125, 2, 2, 128), shape(3, 125, 256)),
        in_specs=vmem(7),
        out_specs=(HBM, HBM, vmem(1)[0]),
        scratch_shapes=[
            pltpu.VMEM((9000, 128), F32),
            pltpu.VMEM((360, 128), F32),
            pltpu.SemaphoreType.DMA((4,)),
        ],
        compiler_params=pltpu.CompilerParams(vmem_limit_bytes=GRANT),
        name="last",
    )(*keep(u, m, ghosts, codes, a, start, reduced))


def as_rows(x):
    return x.reshape(2, 9, 125, 2, 128).transpose(1, 2, 3, 0, 4).reshape(1125, 2, 2, 128)


def as_array(x):
    return x.reshape(9, 125, 2, 2, 128).transpose(3, 0, 1, 2, 4).reshape(2, 9, 125, 256)


def shards(forward, adjoint, material, counts, send_list, neighbours):
    u0, m, a1, ghosts, earlier, lists, codes = first_call(
        counts, as_rows(forward), as_rows(adjoint), material, send_list, neighbours
    )
    u1 = middle_call(u0, m, ghosts, codes, a1)
    a2, ghosts2, reduced = second_call(u1, m, codes, lists, earlier)
    fw, ad, gradient = last_call(u1, m, ghosts2, codes, a2, u0, reduced)
    return as_array(fw), as_array(ad), gradient


def solution(mesh):
    placed = (
        P("shot", None, None, "dom"),
        P("shot", None, None, "dom"),
        P(None, None, "dom"),
        P("dom"),
        P("dom", None, None),
        P("dom", None),
    )
    return jax.shard_map(
        shards,
        mesh=mesh,
        in_specs=placed,
        out_specs=placed[:3],
        check_vma=False,
    )
```
